32 devices in a mesh: groups: 2 (over x), row: 8 (over z, y), rep: 2 (over core).
Axes of the slice: x: 2, y: 2, z: 4, core: 2. Of those that a mesh axis runs over, the one named last changes fastest.
Arguments:
- features: float32 [16384, 512], P(('groups', 'row')), parts along dimension 0, may hold values from -6 to 6
- weight: float32 [512, 512], replicated, may hold values from -0.25 to 0.25
- cotangent: float32 [16384, 512], P(('groups', 'row')), parts along dimension 0, may hold values from -6 to 6
- tile_vals: float32 [128, 2, 16, 128, 128], P(('groups', 'row'), 'rep'), parts along dimension 0, may hold values from -0.1875 to 0.1875
- col_tile: int32 [128, 2, 16], P(('groups', 'row'), 'rep'), parts along dimension 0, may hold values from 0 to 63, as said below
- counts: int32 [128, 2], P(('groups', 'row'), 'rep'), parts along dimension 0, may hold values from 1 to 16, as said below
Outputs:
- output: float32 [16384, 512], P(('groups', 'row')), parts along dimension 0
- input_grad: float32 [16384, 512], P(('groups', 'row')), parts along dimension 0
- weight_grad: float32 [1024, 512], P('groups'), parts along dimension 0
The draws below stay inside these ranges and needn't reach their ends.
There are 2 independent parts, one for each index of `groups`. The reference program is written for one: setup_inputs(seed, part) draws one part's arguments, and reference() takes and returns one part's arrays. A program takes and returns all parts, laid end to end along the dimension named above; an argument that names none is the same for every part. Nothing has to cross between parts.
Inputs may be any that keep to these rules, and one draw needn't show every extreme that they name: `col_tile`: for row tile i and replica k the 16 column tiles are distinct, and each column tile j has j // 8 = (i // 8 - k * 4 - t) mod 8 for some t below 4. `counts`: slots at or past the count are not part of the graph.
All inputs are finite; a program needn't handle non-finite values.
Results may differ from the reference program's by a relative error of at most 0.0003.
Values sent between devices are 32-bit elements; how exact they have to be, the bound alone decides.
No kernel may reach another device: no remote copies, remote signals or barrier semaphores. Data moves between devices by JAX's collectives and lax.ppermute only.
A program may use at most 256 MiB of HBM per device.

```python
import jax
import jax.numpy as jnp
from jax import lax

F = 512
TILE = 128
TILES_DEV = 8
SLOTS = 16
NTILES = 64
NODES = 8192
N_REP = 2


def draw_col_tile(key, part):
    cycle_size = NTILES // TILES_DEV
    half_size = cycle_size // N_REP
    options = half_size * TILES_DEV
    scores = jax.random.randint(key, (NTILES, N_REP, options), 0, 1 << 20)
    option_ids = jax.lax.broadcasted_iota(jnp.int32, (NTILES, N_REP, options), 2)
    order = jnp.argsort(scores * options + option_ids, axis=2, stable=True).astype(jnp.int32)
    chosen = order[:, :, :SLOTS]
    offset = chosen // TILES_DEV
    within = chosen % TILES_DEV
    row_block = jax.lax.broadcasted_iota(jnp.int32, (NTILES, N_REP, SLOTS), 0) // TILES_DEV
    replica = jax.lax.broadcasted_iota(jnp.int32, (NTILES, N_REP, SLOTS), 1)
    column_block = jnp.mod(row_block - replica * half_size - offset, cycle_size)
    return (column_block * TILES_DEV + within).astype(jnp.int32)


def draw_counts(key, part):
    cycle_size = NTILES // TILES_DEV
    first_key = jax.random.fold_in(key, 11)
    second_key = jax.random.fold_in(key, 12)
    third_key = jax.random.fold_in(key, 13)
    level = jax.random.randint(first_key, (cycle_size,), 1, 5)
    level_rows = jnp.repeat(level, TILES_DEV)
    upper = jnp.minimum(level_rows * SLOTS // 4, SLOTS) + 1
    drawn = jax.random.randint(second_key, (NTILES, N_REP), 1, upper[:, None])
    chosen = jax.random.randint(third_key, (), 0, NTILES * N_REP)
    flat_ids = jax.lax.broadcasted_iota(jnp.int32, (NTILES, N_REP), 0) * N_REP + jax.lax.broadcasted_iota(jnp.int32, (NTILES, N_REP), 1)
    return jnp.where(flat_ids == chosen, SLOTS, drawn).astype(jnp.int32)


def level_of(rng, extent, shards, least, high):
    level = 1.0
    for axis_at, blocks in shards:
        steps = jax.random.uniform(jax.random.fold_in(jax.random.fold_in(rng, 6), axis_at), (blocks,), jnp.float32, least / len(shards), high / len(shards))
        level = level * jnp.repeat(jnp.exp(steps), extent[axis_at] // blocks).reshape((-1,) + (1,) * (len(extent) - 1 - axis_at))
    return level


def normal_values(key, dims, spread, reach, pieces=(), dtype=jnp.bfloat16):
    level = level_of(key, dims, pieces, -0.22, 0.18) if pieces else 1.0
    values = jax.random.normal(key, dims, jnp.float32) * spread * level
    return jnp.minimum(jnp.maximum(values, -reach), reach).astype(dtype)


def setup_inputs(seed: int = 0, part: int = 0) -> dict:
    streams_of = jax.random.split(jax.random.key(seed), 7)
    part_keys = jax.random.split(jax.random.fold_in(streams_of[6], part), 7)
    return {
        "features": normal_values(part_keys[0], (NODES, F), 1.0, 6.0, ((0, 8),), jnp.float32),
        "weight": normal_values(streams_of[1], (F, F), F ** -0.5, 0.25, (), jnp.float32),
        "cotangent": normal_values(part_keys[2], (NODES, F), 1.0, 6.0, ((0, 8),), jnp.float32),
        "tile_vals": normal_values(part_keys[3], (NTILES, N_REP, SLOTS, TILE, TILE), (SLOTS * TILE // 2) ** -0.5, 0.1875, ((0, 8), (1, 2)), jnp.float32),
        "col_tile": draw_col_tile(jax.random.fold_in(jax.random.fold_in(streams_of[6], part), 71), part),
        "counts": draw_counts(jax.random.fold_in(jax.random.fold_in(streams_of[6], part), 71), part),
    }


def reference(features, weight, cotangent, tile_vals, col_tile, counts):
    highest = lax.Precision.HIGHEST
    slot_ids = lax.broadcasted_iota(jnp.int32, (NTILES, N_REP, SLOTS), 2)
    active = (slot_ids < counts[:, :, None]).astype(jnp.float32)
    masked = tile_vals * active[:, :, :, None, None]
    feature_tiles = features.reshape(NTILES, TILE, F)

    def row_product(inputs):
        tile_block, columns = inputs
        gathered = feature_tiles[columns.reshape(-1).astype(jnp.int32)]
        flat_tiles = tile_block.reshape(-1, TILE, TILE)
        return jnp.einsum("sab,sbf->af", flat_tiles, gathered, precision=highest)

    aggregated = lax.map(row_product, (masked, col_tile)).reshape(NODES, F)
    pre = jnp.dot(aggregated, weight, precision=highest, preferred_element_type=jnp.float32)
    sigma = jax.nn.sigmoid(pre)
    output = pre * sigma
    grad_pre = cotangent * sigma * (1.0 + pre * (1.0 - sigma))
    weight_grad = jnp.dot(aggregated.T, grad_pre, precision=highest, preferred_element_type=jnp.float32)
    grad_agg = jnp.dot(grad_pre, weight.T, precision=highest, preferred_element_type=jnp.float32)
    grad_tiles = grad_agg.reshape(NTILES, TILE, F)

    def carry_rows(running, inputs):
        tile_block, columns, grad_tile = inputs
        flat_tiles = tile_block.reshape(-1, TILE, TILE)
        contrib = jnp.einsum("sab,af->sbf", flat_tiles, grad_tile, precision=highest)
        return running.at[columns.reshape(-1).astype(jnp.int32)].add(contrib), None

    start_value = jnp.zeros((NTILES, TILE, F), jnp.float32)
    input_grad, _ = lax.scan(carry_rows, start_value, (masked, col_tile, grad_tiles))
    return output, input_grad.reshape(NODES, F), weight_grad
```

```python
import functools

import jax
import jax.numpy as jnp
from jax import lax
from jax.experimental import pallas as pl
from jax.experimental.pallas import tpu as pltpu
from jax.sharding import PartitionSpec as P

BF16 = jnp.bfloat16
F32 = jnp.float32
VMEM_LIMIT = 56 * 1024 * 1024


def ring_place(index, size):
    if size == 8:
        z, y = index // 2, index % 2
        return z + y * (size - 1 - 2 * z)
    return index


def ring_pairs(size):
    at = {ring_place(i, size): i for i in range(size)}
    ahead = [(at[p], at[(p + 1) % size]) for p in range(size)]
    back = [(b, a) for a, b in ahead]
    return ahead, back


def split_hi_lo(value):
    hi = value.astype(BF16)
    return hi, (value - hi.astype(F32)).astype(BF16)


def dot(a, b, dims=((1,), (0,))):
    return lax.dot_general(a, b, (dims, ((), ())), preferred_element_type=F32)


def params():
    return pltpu.CompilerParams(vmem_limit_bytes=VMEM_LIMIT)


def densify_kernel(first, slots, place_ref, count_ref, own_ref, other_ref, *refs):
    hi_ref, lo_ref = refs[-2:]
    row = first + pl.program_id(0)
    tiles_here = pl.num_programs(0)
    del tiles_here
    hi_ref[...] = jnp.zeros_like(hi_ref)
    lo_ref[...] = jnp.zeros_like(lo_ref)
    tile = own_ref.shape[-1]
    for replica, ref in enumerate((own_ref, other_ref)):

        def body(slot, carry, replica=replica, ref=ref):
            hi, lo = split_hi_lo(ref[0, slot])
            block = place_ref[replica, 0, row, slot]
            column = pl.multiple_of(place_ref[replica, 1, row, slot] * tile, tile)
            hi_ref[block, :, pl.ds(column, tile)] = hi
            lo_ref[block, :, pl.ds(column, tile)] = lo
            return carry

        lax.fori_loop(0, count_ref[replica, row], body, 0)


def densify(tiles, place, count, size, pieces):
    own, other = tiles
    tiles_here, slots, tile, _ = own.shape
    rows = tiles_here * tile
    per_call = tiles_here // pieces
    shape = jax.ShapeDtypeStruct((size, rows, rows), BF16)
    dense = ()
    for piece in range(pieces):
        first = piece * per_call
        tile_spec = pl.BlockSpec(
            (1, slots, tile, tile), lambda i, *_, first=first: (first + i, 0, 0, 0)
        )
        out_spec = pl.BlockSpec((size, tile, rows), lambda i, *_, first=first: (0, first + i, 0))
        keep = [pl.BlockSpec(memory_space=pl.ANY)] * len(dense)
        dense = pl.pallas_call(
            functools.partial(densify_kernel, first, slots),
            out_shape=(shape, shape),
            grid_spec=pltpu.PrefetchScalarGridSpec(
                num_scalar_prefetch=2,
                grid=(per_call,),
                in_specs=[tile_spec, tile_spec] + keep,
                out_specs=(out_spec, out_spec),
            ),
            input_output_aliases={4: 0, 5: 1} if dense else {},
            compiler_params=params(),
            cost_estimate=pl.CostEstimate(
                flops=0,
                transcendentals=0,
                bytes_accessed=per_call * tile * (slots * tile * 8 + size * rows * 4),
            ),
            name="densify",
        )(place, count, own, other, *dense)
    return dense


def gather_kernel(blocks, *refs):
    x_refs = refs[: 2 * blocks]
    a_refs = refs[2 * blocks : 4 * blocks]
    rest = refs[4 * blocks :]
    total_ref = rest[0] if len(rest) == 3 else None
    out_ref, x_split = rest[-2:]
    half, width = x_refs[0].shape

    @pl.when(pl.program_id(0) == 0)
    def _():
        for n in range(2 * blocks):
            hi, lo = split_hi_lo(x_refs[n][...])
            x_split[pl.ds(n * half, half), pl.ds(0, width)] = hi
            x_split[pl.ds(n * half, half), pl.ds(width, width)] = lo

    acc = None
    for n in range(blocks):
        span = pl.ds(n * 2 * half, 2 * half)
        both = dot(a_refs[2 * n][0], x_split[span, :])
        low = dot(a_refs[2 * n + 1][0], x_split[span, pl.ds(0, width)])
        part = both[:, :width] + both[:, width:] + low
        acc = part if acc is None else acc + part
    if total_ref is not None:
        acc = acc + total_ref[...]
    out_ref[...] = acc


def gather_product(dense, chunks, total):
    size, rows, columns = dense[0].shape
    half, width = chunks[0][1].shape
    blocks = len(chunks)
    step = 256
    full = pl.BlockSpec((half, width), lambda i: (0, 0))
    in_specs = [full] * (2 * blocks)
    operands = [value for _, top, bottom in chunks for value in (top, bottom)]
    for block, _, _ in chunks:
        spec = pl.BlockSpec((1, step, columns), lambda i, block=block: (block, i, 0))
        in_specs += [spec, spec]
        operands += [dense[0], dense[1]]
    row_spec = pl.BlockSpec((step, width), lambda i: (i, 0))
    if total is not None:
        in_specs.append(row_spec)
        operands.append(total)
    return pl.pallas_call(
        functools.partial(gather_kernel, blocks),
        out_shape=jax.ShapeDtypeStruct((rows, width), F32),
        grid=(rows // step,),
        in_specs=in_specs,
        out_specs=row_spec,
        scratch_shapes=[pltpu.VMEM((blocks * 2 * half, 2 * width), BF16)],
        compiler_params=params(),
        cost_estimate=pl.CostEstimate(
            flops=6 * blocks * rows * columns * width,
            transcendentals=0,
            bytes_accessed=blocks * (rows * columns * 4 + columns * width * 4) + rows * width * 8,
        ),
        name="gather_product",
    )(*operands)


def layer_kernel(own_ref, other_ref, cot_ref, whi_ref, wlo_ref, out_ref, slope_ref, grad_ref):
    width = own_ref.shape[1]
    own_hi, own_lo = split_hi_lo(own_ref[...])
    other_hi, other_lo = split_hi_lo(other_ref[...])
    top, bottom = pl.ds(0, width), pl.ds(width, width)
    pre = dot(own_hi, whi_ref[top, :]) + dot(other_hi, whi_ref[bottom, :])
    pre += dot(own_lo, whi_ref[top, :]) + dot(other_lo, whi_ref[bottom, :])
    pre += dot(own_hi, wlo_ref[top, :]) + dot(other_hi, wlo_ref[bottom, :])
    sigma = jax.nn.sigmoid(pre)
    out_ref[...] = pre * sigma
    grad_pre = cot_ref[...] * (sigma * (1.0 + pre * (1.0 - sigma)))
    slope_ref[...] = grad_pre
    hi, lo = split_hi_lo(grad_pre)
    turned = ((1,), (1,))
    grad = dot(whi_ref[top, :], hi, turned) + dot(whi_ref[top, :], lo, turned)
    grad += dot(wlo_ref[top, :], hi, turned)
    hi, lo = split_hi_lo(grad)
    grad_ref[pl.ds(0, width), :] = hi
    grad_ref[pl.ds(width, width), :] = lo


def layer(own, other, cotangent, w_hi, w_lo):
    rows, width = own.shape
    features = cotangent.shape[1]
    step = 256
    half_spec = pl.BlockSpec((step, width), lambda i: (i, 0))
    full_spec = pl.BlockSpec((step, features), lambda i: (i, 0))
    weight_spec = pl.BlockSpec(w_hi.shape, lambda i: (0, 0))
    return pl.pallas_call(
        layer_kernel,
        out_shape=(
            jax.ShapeDtypeStruct((rows, features), F32),
            jax.ShapeDtypeStruct((rows, features), F32),
            jax.ShapeDtypeStruct((2 * width, rows), BF16),
        ),
        grid=(rows // step,),
        in_specs=[half_spec, half_spec, full_spec, weight_spec, weight_spec],
        out_specs=(full_spec, full_spec, pl.BlockSpec((2 * width, step), lambda i: (0, i))),
        compiler_params=params(),
        cost_estimate=pl.CostEstimate(
            flops=6 * rows * features * (features + width),
            transcendentals=rows * features,
            bytes_accessed=rows * features * 20,
        ),
        name="layer",
    )(own, other, cotangent, w_hi, w_lo)


def scatter_kernel(turn, grad_ref, hi_ref, lo_ref, *refs):
    out_ref = refs[-1]
    width = grad_ref.shape[0] // 2
    both = dot(grad_ref[...], hi_ref[0])
    acc = both[:width] + both[width:] + dot(grad_ref[pl.ds(0, width), :], lo_ref[0])
    if len(refs) == 2:
        acc = acc + refs[0][...]
    out_ref[...] = acc.T if turn else acc


def scatter_product(dense, grad, block, part, parts, carried, turn):
    size, rows, columns = dense[0].shape
    width = grad.shape[0] // 2
    here = columns // parts
    step = 256
    first = part * (here // step)
    a_spec = pl.BlockSpec((1, rows, step), lambda i: (block, 0, first + i))
    in_specs = [pl.BlockSpec(grad.shape, lambda i: (0, 0)), a_spec, a_spec]
    operands = [grad, dense[0], dense[1]]
    if carried is not None:
        in_specs.append(pl.BlockSpec((width, step), lambda i: (0, i)))
        operands.append(carried)
    if turn:
        out_shape, out_spec = (here, width), pl.BlockSpec((step, width), lambda i: (i, 0))
    else:
        out_shape, out_spec = (width, here), pl.BlockSpec((width, step), lambda i: (0, i))
    return pl.pallas_call(
        functools.partial(scatter_kernel, turn),
        out_shape=jax.ShapeDtypeStruct(out_shape, F32),
        grid=(here // step,),
        in_specs=in_specs,
        out_specs=out_spec,
        compiler_params=params(),
        cost_estimate=pl.CostEstimate(
            flops=6 * rows * here * width,
            transcendentals=0,
            bytes_accessed=rows * here * 4 + rows * width * 4 + here * width * 8,
        ),
        name="scatter_product",
    )(*operands)


def sum_over_row(value, size):
    me = lax.axis_index("row")
    half = value.shape[0] // 2
    odd = me % 2

    def swap(block, distance):
        return lax.ppermute(block, "row", [(i, i ^ distance) for i in range(size)])

    top, bottom = value[:half], value[half:]
    mine = jnp.where(odd == 0, top, bottom)
    sent = jnp.where(odd == 0, bottom, top)
    mine = mine + swap(sent, 1)
    distance = 2
    while distance < size:
        mine = mine + swap(mine, distance)
        distance *= 2
    theirs = swap(mine, 1)
    low = jnp.where(odd == 0, mine, theirs)
    high = jnp.where(odd == 0, theirs, mine)
    return jnp.concatenate([low, high], 0)


def per_device(features, weight, cotangent, tile_vals, col_tile, counts):
    size = lax.axis_size("row")
    hops = size // 2
    rep = lax.axis_index("rep")
    row = lax.axis_index("row")
    tiles_here = tile_vals.shape[0]
    width = features.shape[1] // 2
    half = features.shape[0] // 2
    ahead, back = ring_pairs(size)

    def forth(block):
        return lax.ppermute(block, "row", ahead)

    def rear(block):
        return lax.ppermute(block, "row", back)

    def swap(block):
        return lax.ppermute(block, "rep", [(0, 1), (1, 0)])

    def order(own, other, axis):
        low = jnp.where(rep == 0, own, other)
        high = jnp.where(rep == 0, other, own)
        return jnp.concatenate([low, high], axis)

    mine = jnp.where(rep == 0, features[:, :width], features[:, width:])
    top, bottom = mine[:half], mine[half:]

    got = [{0: (top, bottom)}]
    forward_top, forward_bottom, rear_top, rear_bottom = top, bottom, top, bottom
    for hop in range(1, hops + 1):
        forward_top = forth(forward_top)
        rear_bottom = rear(rear_bottom)
        if hop < hops:
            forward_bottom = forth(forward_bottom)
            rear_top = rear(rear_top)
            got.append(
                {size - hop: (forward_top, forward_bottom), hop: (rear_top, rear_bottom)}
            )
        else:
            got.append({hop: (forward_top, rear_bottom)})

    own_tiles = tile_vals[:, 0]
    other_tiles = swap(own_tiles)
    own_columns = col_tile[:, 0]
    columns = jnp.stack([own_columns, swap(own_columns)])
    block = jnp.mod(ring_place(columns // tiles_here, size) - ring_place(row, size), size)
    place = jnp.stack([block, columns % tiles_here], 1)
    count = jnp.stack([counts[:, 0], swap(counts[:, 0])])
    dense = densify((own_tiles, other_tiles), place, count, size, 4)

    w_own = jnp.where(rep == 0, weight[:width], weight[width:])
    w_other = jnp.where(rep == 0, weight[width:], weight[:width])
    w_rows = jnp.concatenate([w_own, w_other], 0)
    w_high = lax.reduce_precision(w_rows, 8, 7)
    w_hi, w_lo = w_high.astype(BF16), (w_rows - w_high).astype(BF16)

    total = None
    for arrived in got:
        chunks = [(block, first, second) for block, (first, second) in arrived.items()]
        total = gather_product(dense, chunks, total)
    output, grad_pre, grad = layer(total, swap(total), cotangent, w_hi, w_lo)

    def product(block, part, carried=None, turn=False):
        return scatter_product(dense, grad, block, part, 2, carried, turn)

    forward_top = rear_bottom = forward_bottom = rear_top = None
    for hop in range(hops, 0, -1):
        turn = hop == 1
        if hop < hops:
            forward_bottom = forth(product(hop, 1, forward_bottom, turn))
            rear_top = rear(product(size - hop, 0, rear_top, turn))
        forward_top = forth(product(hop, 0, forward_top, turn))
        rear_bottom = rear(product(size - hop, 1, rear_bottom, turn))

    weight_part = lax.dot_general(
        total,
        grad_pre,
        (((0,), (0,)), ((), ())),
        precision=lax.Precision.HIGH,
        preferred_element_type=F32,
    )
    weight_half = sum_over_row(weight_part, size)
    weight_grad = order(weight_half, swap(weight_half), 0)

    home_top = product(0, 0, None, True) + forward_top + rear_top
    home_bottom = product(0, 1, None, True) + forward_bottom + rear_bottom
    input_grad = jnp.concatenate(
        [order(home_top, swap(home_top), 1), order(home_bottom, swap(home_bottom), 1)], 0
    )
    return (output, input_grad, weight_grad)


def solution(mesh):
    return jax.shard_map(
        per_device,
        mesh=mesh,
        in_specs=(
            P(("groups", "row"), None),
            P(),
            P(("groups", "row"), None),
            P(("groups", "row"), "rep", None, None, None),
            P(("groups", "row"), "rep", None),
            P(("groups", "row"), "rep"),
        ),
        out_specs=(P(("groups", "row"), None), P(("groups", "row"), None), P("groups", None)),
        check_vma=False,
    )
```

```python
import functools

import jax
import jax.numpy as jnp
from jax import lax
from jax.experimental import pallas as pl
from jax.experimental.pallas import tpu as pltpu
from jax.sharding import PartitionSpec as P

BF16 = jnp.bfloat16
F32 = jnp.float32


def ring_place(index, size):
    if size == 8:
        z, y = index // 2, index % 2
        return z + y * (size - 1 - 2 * z)
    return index


def ring_pairs(size):
    at = {ring_place(i, size): i for i in range(size)}
    ahead = [(at[p], at[(p + 1) % size]) for p in range(size)]
    back = [(b, a) for a, b in ahead]
    return ahead, back


def split_hi_lo(value):
    hi = value.astype(BF16)
    return hi, (value - hi.astype(F32)).astype(BF16)


def dot(a, b, dims=((1,), (0,))):
    return lax.dot_general(a, b, (dims, ((), ())), preferred_element_type=F32)


def params(mib):
    return pltpu.CompilerParams(vmem_limit_bytes=mib * 1024 * 1024)


def after(value, *others):
    return lax.optimization_barrier((value, *others))[0]


def densify_kernel(first, place_ref, count_ref, own_ref, other_ref, *refs):
    hi_ref, lo_ref = refs[-2:]
    row = first + pl.program_id(0)
    hi_ref[...] = jnp.zeros_like(hi_ref)
    lo_ref[...] = jnp.zeros_like(lo_ref)
    tile = own_ref.shape[-1]
    for replica, ref in enumerate((own_ref, other_ref)):

        def body(slot, carry, replica=replica, ref=ref):
            hi, lo = split_hi_lo(ref[0, slot])
            block = place_ref[replica, 0, row, slot]
            column = pl.multiple_of(place_ref[replica, 1, row, slot] * tile, tile)
            hi_ref[block, :, pl.ds(column, tile)] = hi
            lo_ref[block, :, pl.ds(column, tile)] = lo
            return carry

        lax.fori_loop(0, count_ref[replica, row], body, 0)


def densify(dense, tiles, place, count, size, first, last):
    own, other = tiles
    tiles_here, slots, tile, _ = own.shape
    rows = tiles_here * tile
    shape = jax.ShapeDtypeStruct((size, rows, rows), BF16)
    tile_spec = pl.BlockSpec((1, slots, tile, tile), lambda i, *_: (first + i, 0, 0, 0))
    out_spec = pl.BlockSpec((size, tile, rows), lambda i, *_: (0, first + i, 0))
    return pl.pallas_call(
        functools.partial(densify_kernel, first),
        out_shape=(shape, shape),
        grid_spec=pltpu.PrefetchScalarGridSpec(
            num_scalar_prefetch=2,
            grid=(last - first,),
            in_specs=[tile_spec, tile_spec] + [pl.BlockSpec(memory_space=pl.ANY)] * len(dense),
            out_specs=(out_spec, out_spec),
        ),
        input_output_aliases={4: 0, 5: 1} if dense else {},
        compiler_params=params(50),
        cost_estimate=pl.CostEstimate(
            flops=0,
            transcendentals=0,
            bytes_accessed=(last - first) * tile * (slots * tile * 8 + size * rows * 4),
        ),
        name="densify",
    )(place, count, own, other, *dense)


def gather_kernel(blocks, *refs):
    x_refs = refs[: 2 * blocks]
    a_refs = refs[2 * blocks : 4 * blocks]
    rest = refs[4 * blocks :]
    total_ref = rest[0] if len(rest) == 3 else None
    out_ref, x_split = rest[-2:]
    half, width = x_refs[0].shape

    @pl.when(pl.program_id(0) == 0)
    def _():
        for n in range(2 * blocks):
            hi, lo = split_hi_lo(x_refs[n][...])
            x_split[pl.ds(n * half, half), pl.ds(0, width)] = hi
            x_split[pl.ds(n * half, half), pl.ds(width, width)] = lo

    acc = None
    for n in range(blocks):
        span = pl.ds(n * 2 * half, 2 * half)
        both = dot(a_refs[2 * n][0], x_split[span, :])
        low = dot(a_refs[2 * n + 1][0], x_split[span, pl.ds(0, width)])
        part = both[:, :width] + both[:, width:] + low
        acc = part if acc is None else acc + part
    if total_ref is not None:
        acc = acc + total_ref[...]
    out_ref[...] = acc


def gather_product(dense, chunks, total):
    size, rows, columns = dense[0].shape
    half, width = chunks[0][1].shape
    blocks = len(chunks)
    step = rows // 2
    full = pl.BlockSpec((half, width), lambda i: (0, 0))
    in_specs = [full] * (2 * blocks)
    operands = [value for _, top, bottom in chunks for value in (top, bottom)]
    for block, _, _ in chunks:
        spec = pl.BlockSpec((1, step, columns), lambda i, block=block: (block, i, 0))
        in_specs += [spec, spec]
        operands += [dense[0], dense[1]]
    row_spec = pl.BlockSpec((step, width), lambda i: (i, 0))
    if total is not None:
        in_specs.append(row_spec)
        operands.append(total)
    return pl.pallas_call(
        functools.partial(gather_kernel, blocks),
        out_shape=jax.ShapeDtypeStruct((rows, width), F32),
        grid=(rows // step,),
        in_specs=in_specs,
        out_specs=row_spec,
        scratch_shapes=[pltpu.VMEM((blocks * 2 * half, 2 * width), BF16)],
        compiler_params=params(50),
        cost_estimate=pl.CostEstimate(
            flops=6 * blocks * rows * columns * width,
            transcendentals=0,
            bytes_accessed=blocks * (rows * columns * 4 + columns * width * 4) + rows * width * 8,
        ),
        name="gather_product",
    )(*operands)


def layer_kernel(*refs):
    x_refs = refs[:4]
    hi_ref, lo_ref, own_ref, other_ref, cot_ref, whi_ref, wlo_ref = refs[4:11]
    out_ref, pre_grad_ref, total_ref, grad_ref, top_ref, bottom_ref, x_split = refs[11:]
    half, width = x_refs[0].shape
    both_width = 2 * width

    @pl.when(pl.program_id(0) == 0)
    def _():
        for n in range(4):
            hi, lo = split_hi_lo(x_refs[n][...])
            span = pl.ds((n % 2) * half, half)
            x_split[span, pl.ds((n // 2) * width, width)] = hi
            x_split[span, pl.ds(both_width + (n // 2) * width, width)] = lo

    a_hi, a_lo = hi_ref[0], lo_ref[0]
    both = dot(a_hi, x_split[...])
    total = both[:, :both_width] + both[:, both_width:] + dot(a_lo, x_split[:, pl.ds(0, both_width)])
    total = total + jnp.concatenate([own_ref[...], other_ref[...]], 1)
    total_ref[...] = total[:, :width]
    hi, lo = split_hi_lo(total)
    pre = dot(hi, whi_ref[...]) + dot(lo, whi_ref[...]) + dot(hi, wlo_ref[...])
    sigma = jax.nn.sigmoid(pre)
    out_ref[...] = pre * sigma
    pre_grad = cot_ref[...] * (sigma * (1.0 + pre * (1.0 - sigma)))
    pre_grad_ref[...] = pre_grad
    hi, lo = split_hi_lo(pre_grad)
    mine = pl.ds(0, width)
    turned = ((1,), (1,))
    grad = dot(hi, whi_ref[mine, :], turned) + dot(lo, whi_ref[mine, :], turned)
    grad += dot(hi, wlo_ref[mine, :], turned)
    hi, lo = split_hi_lo(grad)
    grad = jnp.concatenate([hi, lo], 1)
    grad_ref[...] = grad
    down = ((0,), (0,))
    both = dot(a_hi, grad, down)
    part = both[:, :width] + both[:, width:] + dot(a_lo, hi, down)

    @pl.when(pl.program_id(0) == 0)
    def _():
        top_ref[...] = part[:half]
        bottom_ref[...] = part[half:]

    @pl.when(pl.program_id(0) != 0)
    def _():
        top_ref[...] += part[:half]
        bottom_ref[...] += part[half:]


def layer(dense, block, x_own, x_other, own, other, cotangent, w_hi, w_lo):
    size, rows, columns = dense[0].shape
    width = own.shape[1]
    half = x_own[0].shape[0]
    features = cotangent.shape[1]
    step = 256
    x_spec = pl.BlockSpec((half, width), lambda i: (0, 0))
    a_spec = pl.BlockSpec((1, step, columns), lambda i: (block, i, 0))
    half_spec = pl.BlockSpec((step, width), lambda i: (i, 0))
    full_spec = pl.BlockSpec((step, features), lambda i: (i, 0))
    weight_spec = pl.BlockSpec(w_hi.shape, lambda i: (0, 0))
    return pl.pallas_call(
        layer_kernel,
        out_shape=(
            jax.ShapeDtypeStruct((rows, features), F32),
            jax.ShapeDtypeStruct((rows, features), F32),
            jax.ShapeDtypeStruct((rows, width), F32),
            jax.ShapeDtypeStruct((rows, 2 * width), BF16),
            jax.ShapeDtypeStruct((half, width), F32),
            jax.ShapeDtypeStruct((half, width), F32),
        ),
        grid=(rows // step,),
        in_specs=[x_spec] * 4
        + [a_spec, a_spec, half_spec, half_spec, full_spec, weight_spec, weight_spec],
        out_specs=(
            full_spec,
            full_spec,
            half_spec,
            pl.BlockSpec((step, 2 * width), lambda i: (i, 0)),
            x_spec,
            x_spec,
        ),
        scratch_shapes=[pltpu.VMEM((2 * half, 4 * width), BF16)],
        compiler_params=params(50),
        cost_estimate=pl.CostEstimate(
            flops=6 * rows * (3 * columns * width + features * (features + width)),
            transcendentals=rows * features,
            bytes_accessed=rows * (features * 24 + columns * 4),
        ),
        name="layer",
    )(*x_own, *x_other, dense[0], dense[1], own, other, cotangent, w_hi, w_lo)


def scatter_kernel(grad_ref, hi_ref, lo_ref, top_ref, bottom_ref):
    width = grad_ref.shape[1] // 2
    down = ((0,), (0,))
    both = dot(hi_ref[0], grad_ref[...], down)
    part = both[:, :width] + both[:, width:]
    part += dot(lo_ref[0], grad_ref[:, pl.ds(0, width)], down)

    @pl.when(pl.program_id(0) == 0)
    def _():
        top_ref[...] = part

    @pl.when(pl.program_id(0) == 1)
    def _():
        bottom_ref[...] = part


def scatter_product(dense, grad, block):
    size, rows, columns = dense[0].shape
    width = grad.shape[1] // 2
    half = columns // 2
    a_spec = pl.BlockSpec((1, rows, half), lambda i: (block, 0, i))
    out_spec = pl.BlockSpec((half, width), lambda i: (0, 0))
    shape = jax.ShapeDtypeStruct((half, width), F32)
    return pl.pallas_call(
        scatter_kernel,
        out_shape=(shape, shape),
        grid=(2,),
        in_specs=[pl.BlockSpec(grad.shape, lambda i: (0, 0)), a_spec, a_spec],
        out_specs=(out_spec, out_spec),
        compiler_params=params(50),
        cost_estimate=pl.CostEstimate(
            flops=6 * rows * columns * width,
            transcendentals=0,
            bytes_accessed=rows * columns * 4 + rows * width * 4 + columns * width * 4,
        ),
        name="scatter_product",
    )(grad, dense[0], dense[1])


def sum_over_row(value, size):
    me = lax.axis_index("row")
    half = value.shape[0] // 2
    odd = me % 2

    def swap(block, distance):
        return lax.ppermute(block, "row", [(i, i ^ distance) for i in range(size)])

    top, bottom = value[:half], value[half:]
    mine = jnp.where(odd == 0, top, bottom)
    sent = jnp.where(odd == 0, bottom, top)
    mine = mine + swap(sent, 1)
    distance = 2
    while distance < size:
        mine = mine + swap(mine, distance)
        distance *= 2
    theirs = swap(mine, 1)
    low = jnp.where(odd == 0, mine, theirs)
    high = jnp.where(odd == 0, theirs, mine)
    return jnp.concatenate([low, high], 0)


def per_device(features, weight, cotangent, tile_vals, col_tile, counts):
    size = lax.axis_size("row")
    hops = size // 2
    rep = lax.axis_index("rep")
    row = lax.axis_index("row")
    tiles_here = tile_vals.shape[0]
    width = features.shape[1] // 2
    half = features.shape[0] // 2
    ahead, back = ring_pairs(size)

    def forth(block):
        return lax.ppermute(block, "row", ahead)

    def rear(block):
        return lax.ppermute(block, "row", back)

    def swap(block):
        return lax.ppermute(block, "rep", [(0, 1), (1, 0)])

    def order(own, other, axis):
        low = jnp.where(rep == 0, own, other)
        high = jnp.where(rep == 0, other, own)
        return jnp.concatenate([low, high], axis)

    own_tiles = tile_vals[:, 0]
    other_tiles = swap(own_tiles)
    own_columns = col_tile[:, 0]
    columns = jnp.stack([own_columns, swap(own_columns)])
    block = jnp.mod(ring_place(columns // tiles_here, size) - ring_place(row, size), size)
    place = jnp.stack([block, columns % tiles_here], 1)
    count = jnp.stack([counts[:, 0], swap(counts[:, 0])])

    w_own = jnp.where(rep == 0, weight[:width], weight[width:])
    w_other = jnp.where(rep == 0, weight[width:], weight[:width])
    w_rows = jnp.concatenate([w_own, w_other], 0)
    w_high = lax.reduce_precision(w_rows, 8, 7)
    w_hi, w_lo = w_high.astype(BF16), (w_rows - w_high).astype(BF16)

    mine = jnp.where(rep == 0, features[:, :width], features[:, width:])
    top, bottom = mine[:half], mine[half:]
    dense, total = (), None
    cuts = [0, tiles_here * 3 // 8, tiles_here * 3 // 4, tiles_here]
    ready = []

    def next_piece():
        nonlocal dense
        done = next_piece.done
        if done < 3:
            dense = densify(
                dense, (own_tiles, other_tiles), place, count, size, cuts[done], cuts[done + 1]
            )
            next_piece.done += 1
            if next_piece.done < 3:
                return dense
        return multiply_ready()

    next_piece.done = 0

    def multiply_ready():
        nonlocal total
        if next_piece.done == 3 and ready:
            total = gather_product(dense, ready.pop(0), total)
            return (total,)
        return ()

    ready.append([(0, top, bottom)])
    forward_top, forward_bottom, rear_top, rear_bottom = top, bottom, top, bottom
    covered = ()
    for hop in range(1, hops + 1):
        if hop > 2:
            covered = next_piece()
        if covered:
            forward_top, rear_bottom = (after(v, *covered) for v in (forward_top, rear_bottom))
        forward_top = forth(forward_top)
        rear_bottom = rear(rear_bottom)
        if hop < hops:
            if hop > 1:
                covered = next_piece()
                forward_bottom, rear_top = (after(v, *covered) for v in (forward_bottom, rear_top))
            forward_bottom = forth(forward_bottom)
            rear_top = rear(rear_top)
            ready.append(
                [(size - hop, forward_top, forward_bottom), (hop, rear_top, rear_bottom)]
            )
    while ready:
        multiply_ready()
    x_last = (forward_top, rear_bottom)
    other_total = swap(total)
    x_other = tuple(swap(v) for v in x_last)
    output, grad_pre, total, grad, first_top, first_bottom = layer(
        dense, hops, x_last, x_other, total, other_total, cotangent, w_hi, w_lo
    )

    def product(block):
        return scatter_product(dense, grad, block)

    forward_top, rear_bottom = forth(first_top), rear(first_bottom)
    forward_bottom = rear_top = None
    for hop in range(hops - 1, 0, -1):
        ahead_top, ahead_bottom = product(hop)
        back_top, back_bottom = product(size - hop)
        if forward_bottom is not None:
            ahead_bottom = ahead_bottom + forward_bottom
            back_top = back_top + rear_top
        forward_bottom = forth(ahead_bottom)
        rear_top = rear(back_top)
        forward_top = forth(ahead_top + forward_top)
        rear_bottom = rear(back_bottom + rear_bottom)

    weight_part = lax.dot_general(
        total,
        grad_pre,
        (((0,), (0,)), ((), ())),
        precision=lax.Precision.HIGH,
        preferred_element_type=F32,
    )
    weight_half = sum_over_row(weight_part, size)
    weight_grad = order(weight_half, swap(weight_half), 0)

    home_top, home_bottom = product(0)
    home_top = home_top + forward_top + rear_top
    home_bottom = home_bottom + forward_bottom + rear_bottom
    input_grad = jnp.concatenate(
        [order(home_top, swap(home_top), 1), order(home_bottom, swap(home_bottom), 1)], 0
    )
    return (output, input_grad, weight_grad)


def solution(mesh):
    return jax.shard_map(
        per_device,
        mesh=mesh,
        in_specs=(
            P(("groups", "row"), None),
            P(),
            P(("groups", "row"), None),
            P(("groups", "row"), "rep", None, None, None),
            P(("groups", "row"), "rep", None),
            P(("groups", "row"), "rep"),
        ),
        out_specs=(P(("groups", "row"), None), P(("groups", "row"), None), P("groups", None)),
        check_vma=False,
    )
```

```python
import functools

import jax
import jax.numpy as jnp
from jax import lax
from jax.experimental import pallas as pl
from jax.experimental.pallas import tpu as pltpu
from jax.sharding import PartitionSpec as P

BF16 = jnp.bfloat16
F32 = jnp.float32
MIB = 48
SP_FLOPS = [10000000000,1,10000000000,1,10000000000,1,10000000000]
LAYER_MIB = 40
SMALL = pl.CostEstimate(flops=10_000_000_000, transcendentals=0, bytes_accessed=8_000_000)


def ring_place(index, size):
    if size == 8:
        z, y = index // 2, index % 2
        return z + y * (size - 1 - 2 * z)
    return index


def ring_pairs(size):
    at = {ring_place(i, size): i for i in range(size)}
    ahead = [(at[p], at[(p + 1) % size]) for p in range(size)]
    back = [(b, a) for a, b in ahead]
    return ahead, back


def split_hi_lo(value):
    hi = value.astype(BF16)
    return hi, (value - hi.astype(F32)).astype(BF16)


def dot(a, b, dims=((1,), (0,))):
    return lax.dot_general(a, b, (dims, ((), ())), preferred_element_type=F32)


def params(mib):
    return pltpu.CompilerParams(vmem_limit_bytes=mib * 1024 * 1024)


def after(value, *others):
    return lax.optimization_barrier((value, *others))[0]


def densify_kernel(first, far, place_ref, count_ref, own_ref, other_ref, *refs):
    hi_ref, lo_ref, far_hi_ref, far_lo_ref = refs[-4:]
    row = first + pl.program_id(0)
    hi_ref[...] = jnp.zeros_like(hi_ref)
    lo_ref[...] = jnp.zeros_like(lo_ref)
    tile = own_ref.shape[-1]
    for replica, ref in enumerate((own_ref, other_ref)):

        def body(slot, carry, replica=replica, ref=ref):
            hi, lo = split_hi_lo(ref[0, slot])
            block = place_ref[replica, 0, row, slot]
            column = pl.multiple_of(place_ref[replica, 1, row, slot] * tile, tile)
            hi_ref[block, :, pl.ds(column, tile)] = hi
            lo_ref[block, :, pl.ds(column, tile)] = lo
            return carry

        lax.fori_loop(0, count_ref[replica, row], body, 0)
    far_hi_ref[...] = hi_ref[far]
    far_lo_ref[...] = lo_ref[far]


def densify(dense, tiles, place, count, size, first, last):
    own, other = tiles
    tiles_here, slots, tile, _ = own.shape
    rows = tiles_here * tile
    shape = jax.ShapeDtypeStruct((size, rows, rows), BF16)
    tile_spec = pl.BlockSpec((1, slots, tile, tile), lambda i, *_: (first + i, 0, 0, 0))
    out_spec = pl.BlockSpec((size, tile, rows), lambda i, *_: (0, first + i, 0))
    far_shape = jax.ShapeDtypeStruct((rows, rows), BF16)
    far_spec = pl.BlockSpec((tile, rows), lambda i, *_: (first + i, 0))
    return pl.pallas_call(
        functools.partial(densify_kernel, first, size // 2),
        out_shape=(shape, shape, far_shape, far_shape),
        grid_spec=pltpu.PrefetchScalarGridSpec(
            num_scalar_prefetch=2,
            grid=(last - first,),
            in_specs=[tile_spec, tile_spec] + [pl.BlockSpec(memory_space=pl.ANY)] * len(dense),
            out_specs=(out_spec, out_spec, far_spec, far_spec),
        ),
        input_output_aliases={4 + n: n for n in range(len(dense))},
        compiler_params=params(MIB),
        cost_estimate=pl.CostEstimate(
            flops=0,
            transcendentals=0,
            bytes_accessed=(last - first) * tile * (slots * tile * 8 + size * rows * 4),
        ),
        name="densify",
    )(place, count, own, other, *dense)


def gather_kernel(blocks, *refs):
    x_refs = refs[: 2 * blocks]
    a_refs = refs[2 * blocks : 4 * blocks]
    rest = refs[4 * blocks :]
    total_ref = rest[0] if len(rest) == 3 else None
    out_ref, x_split = rest[-2:]
    half, width = x_refs[0].shape

    @pl.when(pl.program_id(0) == 0)
    def _():
        for n in range(2 * blocks):
            hi, lo = split_hi_lo(x_refs[n][...])
            x_split[pl.ds(n * half, half), pl.ds(0, width)] = hi
            x_split[pl.ds(n * half, half), pl.ds(width, width)] = lo

    acc = None
    for n in range(blocks):
        span = pl.ds(n * 2 * half, 2 * half)
        both = dot(a_refs[2 * n][0], x_split[span, :])
        low = dot(a_refs[2 * n + 1][0], x_split[span, pl.ds(0, width)])
        part = both[:, :width] + both[:, width:] + low
        acc = part if acc is None else acc + part
    if total_ref is not None:
        acc = acc + total_ref[...]
    out_ref[...] = acc


def gather_product(dense, chunks, total):
    size, rows, columns = dense[0].shape
    half, width = chunks[0][1].shape
    blocks = len(chunks)
    step = rows // 2
    full = pl.BlockSpec((half, width), lambda i: (0, 0))
    in_specs = [full] * (2 * blocks)
    operands = [value for _, top, bottom in chunks for value in (top, bottom)]
    for block, _, _ in chunks:
        spec = pl.BlockSpec((1, step, columns), lambda i, block=block: (block, i, 0))
        in_specs += [spec, spec]
        operands += [dense[0], dense[1]]
    row_spec = pl.BlockSpec((step, width), lambda i: (i, 0))
    if total is not None:
        in_specs.append(row_spec)
        operands.append(total)
    return pl.pallas_call(
        functools.partial(gather_kernel, blocks),
        out_shape=jax.ShapeDtypeStruct((rows, width), F32),
        grid=(rows // step,),
        in_specs=in_specs,
        out_specs=row_spec,
        scratch_shapes=[pltpu.VMEM((blocks * 2 * half, 2 * width), BF16)],
        compiler_params=params(MIB),
        cost_estimate=pl.CostEstimate(
            flops=6 * blocks * rows * columns * width,
            transcendentals=0,
            bytes_accessed=blocks * (rows * columns * 4 + columns * width * 4) + rows * width * 8,
        ),
        name="gather_product",
    )(*operands)


def layer_kernel(*refs):
    odd_ref = refs[0]
    x_refs = refs[1:5]
    hi_ref, lo_ref, own_ref, other_ref, cot_ref, whi_ref, wlo_ref = refs[5:12]
    out_ref, pre_grad_ref, mine_ref, sent_ref, x_split, total_ref = refs[12:]
    half, width = x_refs[0].shape
    rows, columns = hi_ref.shape
    step = 512
    for n in range(4):
        hi, lo = split_hi_lo(x_refs[n][...])
        at, side = (n % 2) * half, pl.ds((n // 2) * width, width)
        x_split[pl.ds(at, half), side] = hi
        x_split[pl.ds(columns + at, half), side] = lo
        x_split[pl.ds(2 * columns + at, half), side] = hi
    for first in range(0, rows, step):
        here = pl.ds(first, step)
        hi, lo = hi_ref[here, :], lo_ref[here, :]
        total = dot(jnp.concatenate([hi, hi, lo], 1), x_split[...])
        total = total + jnp.concatenate([own_ref[here, :], other_ref[here, :]], 1)
        hi, lo = split_hi_lo(total)
        total_ref[here, :] = hi[:, :width]
        total_ref[pl.ds(rows + first, step), :] = lo[:, :width]
        w_hi, w_lo = whi_ref[...], wlo_ref[...]
        pre = dot(
            jnp.concatenate([hi, lo, hi], 1), jnp.concatenate([w_hi, w_hi, w_lo], 0)
        )
        sigma = jax.nn.sigmoid(pre)
        out_ref[here, :] = pre * sigma
        pre_grad = cot_ref[here, :] * (sigma * (1.0 + pre * (1.0 - sigma)))
        hi, lo = split_hi_lo(pre_grad)
        pre_grad_ref[here, :] = hi
        pre_grad_ref[pl.ds(rows + first, step), :] = lo
    value = turned_dot(total_ref[pl.ds(0, rows), :], total_ref[pl.ds(rows, rows), :], pre_grad_ref)
    top, bottom = value[: width // 2], value[width // 2 :]
    odd = odd_ref[0]
    mine_ref[...] = jnp.where(odd == 0, top, bottom)
    sent_ref[...] = jnp.where(odd == 0, bottom, top)


def layer_grad_kernel(*refs):
    pre_grad_ref, hi_ref, lo_ref, whi_ref, wlo_ref, grad_ref, top_ref, bottom_ref = refs
    rows = hi_ref.shape[0]
    half, width = top_ref.shape
    step = 512
    mine = pl.ds(0, width)
    for first in range(0, rows, step):
        hi, lo = pre_grad_ref[pl.ds(first, step), :], pre_grad_ref[pl.ds(rows + first, step), :]
        w_hi, w_lo = whi_ref[mine, :], wlo_ref[mine, :]
        grad = dot(
            jnp.concatenate([hi, lo, hi], 1),
            jnp.concatenate([w_hi, w_hi, w_lo], 1),
            ((1,), (1,)),
        )
        hi, lo = split_hi_lo(grad)
        grad_ref[pl.ds(first, step), :] = hi
        grad_ref[pl.ds(rows + first, step), :] = lo
    for first in range(0, 2 * half, 256):
        part = turned_dot(hi_ref[:, pl.ds(first, 256)], lo_ref[:, pl.ds(first, 256)], grad_ref)
        if first < half:
            top_ref[pl.ds(first, 256), :] = part
        else:
            bottom_ref[pl.ds(first - half, 256), :] = part


def turned_dot(hi, lo, right_ref):
    rows = hi.shape[0]
    right_hi, right_lo = right_ref[pl.ds(0, rows), :], right_ref[pl.ds(rows, rows), :]
    left = jnp.concatenate([hi, hi, lo], 0)
    return dot(left, jnp.concatenate([right_hi, right_lo, right_hi], 0), ((0,), (0,)))


def layer(odd, far, x_own, x_other, own, other, cotangent, w_hi, w_lo):
    rows, columns = far[0].shape
    width = own.shape[1]
    features = cotangent.shape[1]
    whole = pl.BlockSpec(memory_space=pltpu.VMEM)
    return pl.pallas_call(
        layer_kernel,
        out_shape=(
            jax.ShapeDtypeStruct((rows, features), F32),
            jax.ShapeDtypeStruct((2 * rows, features), BF16),
            jax.ShapeDtypeStruct((width // 2, features), F32),
            jax.ShapeDtypeStruct((width // 2, features), F32),
        ),
        in_specs=[pl.BlockSpec(memory_space=pltpu.SMEM)] + [whole] * 11,
        out_specs=(whole,) * 4,
        scratch_shapes=[
            pltpu.VMEM((3 * columns, features), BF16),
            pltpu.VMEM((2 * rows, width), BF16),
        ],
        compiler_params=params(LAYER_MIB),
        cost_estimate=pl.CostEstimate(flops=1, transcendentals=0, bytes_accessed=1),
        name="layer",
    )(odd, *x_own, *x_other, *far, own, other, cotangent, w_hi, w_lo)


def layer_grad(pre_grad, far, w_hi, w_lo):
    rows, columns = far[0].shape
    width = w_hi.shape[0] // 2
    whole = pl.BlockSpec(memory_space=pltpu.VMEM)
    return pl.pallas_call(
        layer_grad_kernel,
        out_shape=(
            jax.ShapeDtypeStruct((2 * rows, width), BF16),
            jax.ShapeDtypeStruct((columns // 2, width), F32),
            jax.ShapeDtypeStruct((columns // 2, width), F32),
        ),
        in_specs=[whole] * 5,
        out_specs=(whole,) * 3,
        compiler_params=params(LAYER_MIB),
        cost_estimate=pl.CostEstimate(flops=1, transcendentals=0, bytes_accessed=1),
        name="layer_grad",
    )(pre_grad, *far, w_hi, w_lo)


def scatter_kernel(*refs):
    grad_ref, hi_ref, lo_ref = refs[:3]
    came, outs = refs[3:-2], refs[-2:]
    part = turned_dot(hi_ref[0], lo_ref[0], grad_ref)
    step = part.shape[0]
    per_side = outs[0].shape[0] // step
    at = pl.program_id(0)
    for side in range(2):

        @pl.when(at // per_side == side)
        def _(side=side):
            here = pl.ds((at % per_side) * step, step)
            outs[side][here, :] = part + came[side][here, :] if came else part


def scatter_product(dense, grad, blocks, parts, carried=()):
    flops = SP_FLOPS[(0 if blocks[0] == 0 else (6 - 2 * blocks[0]) + (2 if parts[0] == 0 else 1)) if dense[0].shape[0] == 8 else 0]
    size, rows, columns = dense[0].shape
    width = grad.shape[1]
    half = columns // 2
    step = 256
    per_side = half // step

    def place(i):
        side = i // per_side
        block = blocks[0] + side * (blocks[1] - blocks[0])
        part = parts[0] + side * (parts[1] - parts[0])
        return (block, 0, part * per_side + i % per_side)

    a_spec = pl.BlockSpec((1, rows, step), place)
    whole = pl.BlockSpec(memory_space=pltpu.VMEM)
    return pl.pallas_call(
        scatter_kernel,
        out_shape=(jax.ShapeDtypeStruct((half, width), F32),) * 2,
        grid=(2 * per_side,),
        in_specs=[whole, a_spec, a_spec] + [whole] * len(carried),
        out_specs=(whole, whole),
        compiler_params=params(MIB),
        cost_estimate=pl.CostEstimate(flops=flops, transcendentals=0, bytes_accessed=1),
        name="scatter_product",
    )(grad, dense[0], dense[1], *carried)


def per_device(features, weight, cotangent, tile_vals, col_tile, counts):
    size = lax.axis_size("row")
    hops = size // 2
    rep = lax.axis_index("rep")
    row = lax.axis_index("row")
    tiles_here = tile_vals.shape[0]
    width = features.shape[1] // 2
    half = features.shape[0] // 2
    ahead, back = ring_pairs(size)

    def forth(block):
        return lax.ppermute(block, "row", ahead)

    def rear(block):
        return lax.ppermute(block, "row", back)

    def swap(block):
        return lax.ppermute(block, "rep", [(0, 1), (1, 0)])

    def order(own, other, axis):
        low = jnp.where(rep == 0, own, other)
        high = jnp.where(rep == 0, other, own)
        return jnp.concatenate([low, high], axis)

    top = lax.dynamic_slice(features, (0, rep * width), (half, width))
    bottom = lax.dynamic_slice(features, (half, rep * width), (half, width))

    own_tiles = tile_vals[:, 0]
    other_tiles = swap(own_tiles)
    first_hop = (forth(top), rear(bottom))
    table = after(jnp.concatenate([col_tile[:, 0], counts], 1), *first_hop)
    tables = jnp.stack([table, swap(table)])
    columns = tables[:, :, :-1]
    block = jnp.mod(ring_place(columns // tiles_here, size) - ring_place(row, size), size)
    place = jnp.stack([block, columns % tiles_here], 1)
    count = tables[:, :, -1]

    w_own = jnp.where(rep == 0, weight[:width], weight[width:])
    w_other = jnp.where(rep == 0, weight[width:], weight[:width])
    w_rows = jnp.concatenate([w_own, w_other], 0)
    w_high = lax.reduce_precision(w_rows, 8, 7)
    w_hi, w_lo = w_high.astype(BF16), (w_rows - w_high).astype(BF16)

    dense, total = (), None
    cuts = [0, tiles_here * 3 // 8, tiles_here * 3 // 4, tiles_here]
    ready = []

    def next_piece():
        nonlocal dense
        done = next_piece.done
        if done < 3:
            dense = densify(
                dense, (own_tiles, other_tiles), place, count, size, cuts[done], cuts[done + 1]
            )
            next_piece.done += 1
            if next_piece.done < 3:
                return dense
        return multiply_ready()

    next_piece.done = 0

    def multiply_ready():
        nonlocal total
        if next_piece.done == 3 and ready:
            total = gather_product(dense[:2], ready.pop(0), total)
            return (total,)
        return ()

    ready.append([(0, top, bottom)])
    forward_top, forward_bottom, rear_top, rear_bottom = top, bottom, top, bottom
    covered = (w_hi, w_lo)
    for hop in range(1, hops + 1):
        if hop > 2:
            covered = next_piece()
        if hop > 1:
            forward_top, rear_bottom = (after(v, *covered) for v in (forward_top, rear_bottom))
            forward_top, rear_bottom = forth(forward_top), rear(rear_bottom)
        else:
            forward_top, rear_bottom = first_hop
        if hop < hops:
            if hop > 1:
                covered = next_piece()
                forward_bottom, rear_top = (after(v, *covered) for v in (forward_bottom, rear_top))
            forward_bottom = forth(forward_bottom)
            rear_top = rear(rear_top)
            ready.append(
                [(size - hop, forward_top, forward_bottom), (hop, rear_top, rear_bottom)]
            )
    while ready:
        multiply_ready()
    x_last = (forward_top, rear_bottom)
    other_total = swap(total)
    x_other = tuple(swap(v) for v in x_last)
    odd = jnp.mod(row, 2)
    output, pre_grad, weight_mine, weight_sent = layer(
        odd.reshape(1), dense[2:], x_last, x_other, total, other_total, cotangent, w_hi, w_lo
    )


    def exchange(block, distance):
        return lax.ppermute(block, "row", [(i, i ^ distance) for i in range(size)])

    weight_mine = weight_mine + exchange(weight_sent, 1)
    distance = 2
    while distance < size:
        weight_mine = weight_mine + exchange(weight_mine, distance)
        distance *= 2
    weight_theirs = exchange(weight_mine, 1)
    low = jnp.where(odd == 0, weight_mine, weight_theirs)
    high = jnp.where(odd == 0, weight_theirs, weight_mine)
    weight_half = jnp.concatenate([low, high], 0)
    grad, first_top, first_bottom = layer_grad(pre_grad, dense[2:], w_hi, w_lo)
    tops = (forth(first_top), rear(first_bottom))
    bottoms = ()
    for hop in range(hops - 1, 0, -1):
        blocks = (hop, size - hop)
        result = scatter_product(dense[:2], grad, blocks, (1, 0), bottoms)
        bottoms = (forth(result[0]), rear(result[1]))
        result = scatter_product(dense[:2], grad, blocks, (0, 1), tops)
        tops = (forth(result[0]), rear(result[1]))
    home_top, home_bottom = scatter_product(dense[:2], after(grad, *result), (0, 0), (0, 1))
    weight_grad = order(weight_half, swap(weight_half), 0)
    home_bottom = home_bottom + bottoms[0] + tops[1]
    home_top = home_top + bottoms[1] + tops[0]
    input_grad = jnp.concatenate(
        [order(home_top, swap(home_top), 1), order(home_bottom, swap(home_bottom), 1)], 0
    )
    return (output, input_grad, weight_grad)


def solution(mesh):
    return jax.shard_map(
        per_device,
        mesh=mesh,
        in_specs=(
            P(("groups", "row"), None),
            P(),
            P(("groups", "row"), None),
            P(("groups", "row"), "rep", None, None, None),
            P(("groups", "row"), "rep", None),
            P(("groups", "row"), "rep"),
        ),
        out_specs=(P(("groups", "row"), None), P(("groups", "row"), None), P("groups", None)),
        check_vma=False,
    )
```

```python
import functools

import jax
import jax.numpy as jnp
from jax import lax
from jax.experimental import pallas as pl
from jax.experimental.pallas import tpu as pltpu
from jax.sharding import PartitionSpec as P

BF16 = jnp.bfloat16
F32 = jnp.float32
MIB = 48
SP_FLOPS = [10000000000,10000000000,10000000000,1,10000000000,1,10000000000]
LAYER_MIB = 40
SMALL = pl.CostEstimate(flops=10_000_000_000, transcendentals=0, bytes_accessed=8_000_000)


def ring_place(index, size):
    if size == 8:
        z, y = index // 2, index % 2
        return z + y * (size - 1 - 2 * z)
    return index


def ring_pairs(size):
    at = {ring_place(i, size): i for i in range(size)}
    ahead = [(at[p], at[(p + 1) % size]) for p in range(size)]
    back = [(b, a) for a, b in ahead]
    return ahead, back


def split_hi_lo(value):
    hi = value.astype(BF16)
    return hi, (value - hi.astype(F32)).astype(BF16)


def dot(a, b, dims=((1,), (0,))):
    return lax.dot_general(a, b, (dims, ((), ())), preferred_element_type=F32)


def params(mib):
    return pltpu.CompilerParams(vmem_limit_bytes=mib * 1024 * 1024)


def after(value, *others):
    return lax.optimization_barrier((value, *others))[0]


def densify_kernel(first, far, place_ref, count_ref, own_ref, other_ref, *refs):
    hi_ref, lo_ref, far_hi_ref, far_lo_ref = refs[-4:]
    row = first + pl.program_id(0)
    hi_ref[...] = jnp.zeros_like(hi_ref)
    lo_ref[...] = jnp.zeros_like(lo_ref)
    tile = own_ref.shape[-1]
    for replica, ref in enumerate((own_ref, other_ref)):

        def body(slot, carry, replica=replica, ref=ref):
            hi, lo = split_hi_lo(ref[0, slot])
            block = place_ref[replica, 0, row, slot]
            column = pl.multiple_of(place_ref[replica, 1, row, slot] * tile, tile)
            hi_ref[block, :, pl.ds(column, tile)] = hi
            lo_ref[block, :, pl.ds(column, tile)] = lo
            return carry

        lax.fori_loop(0, count_ref[replica, row], body, 0)
    far_hi_ref[...] = hi_ref[far]
    far_lo_ref[...] = lo_ref[far]


def densify(dense, tiles, place, count, size, first, last):
    own, other = tiles
    tiles_here, slots, tile, _ = own.shape
    rows = tiles_here * tile
    shape = jax.ShapeDtypeStruct((size, rows, rows), BF16)
    tile_spec = pl.BlockSpec((1, slots, tile, tile), lambda i, *_: (first + i, 0, 0, 0))
    out_spec = pl.BlockSpec((size, tile, rows), lambda i, *_: (0, first + i, 0))
    far_shape = jax.ShapeDtypeStruct((rows, rows), BF16)
    far_spec = pl.BlockSpec((tile, rows), lambda i, *_: (first + i, 0))
    return pl.pallas_call(
        functools.partial(densify_kernel, first, size // 2),
        out_shape=(shape, shape, far_shape, far_shape),
        grid_spec=pltpu.PrefetchScalarGridSpec(
            num_scalar_prefetch=2,
            grid=(last - first,),
            in_specs=[tile_spec, tile_spec] + [pl.BlockSpec(memory_space=pl.ANY)] * len(dense),
            out_specs=(out_spec, out_spec, far_spec, far_spec),
        ),
        input_output_aliases={4 + n: n for n in range(len(dense))},
        compiler_params=params(MIB),
        cost_estimate=pl.CostEstimate(
            flops=0,
            transcendentals=0,
            bytes_accessed=(last - first) * tile * (slots * tile * 8 + size * rows * 4),
        ),
        name="densify",
    )(place, count, own, other, *dense)


def gather_kernel(blocks, *refs):
    x_refs = refs[: 2 * blocks]
    a_refs = refs[2 * blocks : 4 * blocks]
    rest = refs[4 * blocks :]
    total_ref = rest[0] if len(rest) == 3 else None
    out_ref, x_split = rest[-2:]
    half, width = x_refs[0].shape

    @pl.when(pl.program_id(0) == 0)
    def _():
        for n in range(2 * blocks):
            hi, lo = split_hi_lo(x_refs[n][...])
            x_split[pl.ds(n * half, half), pl.ds(0, width)] = hi
            x_split[pl.ds(n * half, half), pl.ds(width, width)] = lo

    acc = None
    for n in range(blocks):
        span = pl.ds(n * 2 * half, 2 * half)
        both = dot(a_refs[2 * n][0], x_split[span, :])
        low = dot(a_refs[2 * n + 1][0], x_split[span, pl.ds(0, width)])
        part = both[:, :width] + both[:, width:] + low
        acc = part if acc is None else acc + part
    if total_ref is not None:
        acc = acc + total_ref[...]
    out_ref[...] = acc


def gather_product(dense, chunks, total):
    size, rows, columns = dense[0].shape
    half, width = chunks[0][1].shape
    blocks = len(chunks)
    step = rows // 2
    full = pl.BlockSpec((half, width), lambda i: (0, 0))
    in_specs = [full] * (2 * blocks)
    operands = [value for _, top, bottom in chunks for value in (top, bottom)]
    for block, _, _ in chunks:
        spec = pl.BlockSpec((1, step, columns), lambda i, block=block: (block, i, 0))
        in_specs += [spec, spec]
        operands += [dense[0], dense[1]]
    row_spec = pl.BlockSpec((step, width), lambda i: (i, 0))
    if total is not None:
        in_specs.append(row_spec)
        operands.append(total)
    return pl.pallas_call(
        functools.partial(gather_kernel, blocks),
        out_shape=jax.ShapeDtypeStruct((rows, width), F32),
        grid=(rows // step,),
        in_specs=in_specs,
        out_specs=row_spec,
        scratch_shapes=[pltpu.VMEM((blocks * 2 * half, 2 * width), BF16)],
        compiler_params=params(MIB),
        cost_estimate=pl.CostEstimate(
            flops=6 * blocks * rows * columns * width,
            transcendentals=0,
            bytes_accessed=blocks * (rows * columns * 4 + columns * width * 4) + rows * width * 8,
        ),
        name="gather_product",
    )(*operands)


def layer_kernel(*refs):
    odd_ref = refs[0]
    x_refs = refs[1:5]
    hi_ref, lo_ref, own_ref, other_ref, cot_ref, whi_ref, wlo_ref = refs[5:12]
    out_ref, pre_grad_ref, mine_ref, sent_ref, x_split, total_ref = refs[12:]
    half, width = x_refs[0].shape
    rows, columns = hi_ref.shape
    step = 512
    for n in range(4):
        hi, lo = split_hi_lo(x_refs[n][...])
        at, side = (n % 2) * half, pl.ds((n // 2) * width, width)
        x_split[pl.ds(at, half), side] = hi
        x_split[pl.ds(columns + at, half), side] = lo
        x_split[pl.ds(2 * columns + at, half), side] = hi
    for first in range(0, rows, step):
        here = pl.ds(first, step)
        hi, lo = hi_ref[here, :], lo_ref[here, :]
        total = dot(jnp.concatenate([hi, hi, lo], 1), x_split[...])
        total = total + jnp.concatenate([own_ref[here, :], other_ref[here, :]], 1)
        hi, lo = split_hi_lo(total)
        total_ref[here, :] = hi[:, :width]
        total_ref[pl.ds(rows + first, step), :] = lo[:, :width]
        w_hi, w_lo = whi_ref[...], wlo_ref[...]
        pre = dot(
            jnp.concatenate([hi, lo, hi], 1), jnp.concatenate([w_hi, w_hi, w_lo], 0)
        )
        sigma = jax.nn.sigmoid(pre)
        out_ref[here, :] = pre * sigma
        pre_grad = cot_ref[here, :] * (sigma * (1.0 + pre * (1.0 - sigma)))
        hi, lo = split_hi_lo(pre_grad)
        pre_grad_ref[here, :] = hi
        pre_grad_ref[pl.ds(rows + first, step), :] = lo
    value = turned_dot(total_ref[pl.ds(0, rows), :], total_ref[pl.ds(rows, rows), :], pre_grad_ref)
    top, bottom = value[: width // 2], value[width // 2 :]
    odd = odd_ref[0]
    mine_ref[...] = jnp.where(odd == 0, top, bottom)
    sent_ref[...] = jnp.where(odd == 0, bottom, top)


def layer_grad_kernel(*refs):
    pre_grad_ref, hi_ref, lo_ref, whi_ref, wlo_ref, grad_ref, top_ref, bottom_ref = refs
    rows = hi_ref.shape[0]
    half, width = top_ref.shape
    step = 512
    mine = pl.ds(0, width)
    for first in range(0, rows, step):
        hi, lo = pre_grad_ref[pl.ds(first, step), :], pre_grad_ref[pl.ds(rows + first, step), :]
        w_hi, w_lo = whi_ref[mine, :], wlo_ref[mine, :]
        grad = dot(
            jnp.concatenate([hi, lo, hi], 1),
            jnp.concatenate([w_hi, w_hi, w_lo], 1),
            ((1,), (1,)),
        )
        hi, lo = split_hi_lo(grad)
        grad_ref[pl.ds(first, step), :] = hi
        grad_ref[pl.ds(rows + first, step), :] = lo
    for first in range(0, 2 * half, 256):
        part = turned_dot(hi_ref[:, pl.ds(first, 256)], lo_ref[:, pl.ds(first, 256)], grad_ref)
        if first < half:
            top_ref[pl.ds(first, 256), :] = part
        else:
            bottom_ref[pl.ds(first - half, 256), :] = part


def turned_dot(hi, lo, right_ref):
    rows = hi.shape[0]
    right_hi, right_lo = right_ref[pl.ds(0, rows), :], right_ref[pl.ds(rows, rows), :]
    left = jnp.concatenate([hi, hi, lo], 0)
    return dot(left, jnp.concatenate([right_hi, right_lo, right_hi], 0), ((0,), (0,)))


def layer(odd, far, x_own, x_other, own, other, cotangent, w_hi, w_lo):
    rows, columns = far[0].shape
    width = own.shape[1]
    features = cotangent.shape[1]
    whole = pl.BlockSpec(memory_space=pltpu.VMEM)
    return pl.pallas_call(
        layer_kernel,
        out_shape=(
            jax.ShapeDtypeStruct((rows, features), F32),
            jax.ShapeDtypeStruct((2 * rows, features), BF16),
            jax.ShapeDtypeStruct((width // 2, features), F32),
            jax.ShapeDtypeStruct((width // 2, features), F32),
        ),
        in_specs=[pl.BlockSpec(memory_space=pltpu.SMEM)] + [whole] * 11,
        out_specs=(whole,) * 4,
        scratch_shapes=[
            pltpu.VMEM((3 * columns, features), BF16),
            pltpu.VMEM((2 * rows, width), BF16),
        ],
        compiler_params=params(LAYER_MIB),
        cost_estimate=pl.CostEstimate(flops=1, transcendentals=0, bytes_accessed=1),
        name="layer",
    )(odd, *x_own, *x_other, *far, own, other, cotangent, w_hi, w_lo)


def layer_grad(pre_grad, far, w_hi, w_lo):
    rows, columns = far[0].shape
    width = w_hi.shape[0] // 2
    whole = pl.BlockSpec(memory_space=pltpu.VMEM)
    return pl.pallas_call(
        layer_grad_kernel,
        out_shape=(
            jax.ShapeDtypeStruct((2 * rows, width), BF16),
            jax.ShapeDtypeStruct((columns // 2, width), F32),
            jax.ShapeDtypeStruct((columns // 2, width), F32),
        ),
        in_specs=[whole] * 5,
        out_specs=(whole,) * 3,
        compiler_params=params(LAYER_MIB),
        cost_estimate=pl.CostEstimate(flops=10000000000, transcendentals=0, bytes_accessed=1),
        name="layer_grad",
    )(pre_grad, *far, w_hi, w_lo)


def scatter_kernel(*refs):
    grad_ref, hi_ref, lo_ref = refs[:3]
    came, outs = refs[3:-2], refs[-2:]
    part = turned_dot(hi_ref[0], lo_ref[0], grad_ref)
    step = part.shape[0]
    per_side = outs[0].shape[0] // step
    at = pl.program_id(0)
    for side in range(2):

        @pl.when(at // per_side == side)
        def _(side=side):
            here = pl.ds((at % per_side) * step, step)
            outs[side][here, :] = part + came[side][here, :] if came else part


def scatter_product(dense, grad, blocks, parts, carried=()):
    flops = SP_FLOPS[(0 if blocks[0] == 0 else (6 - 2 * blocks[0]) + (2 if parts[0] == 0 else 1)) if dense[0].shape[0] == 8 else 0]
    size, rows, columns = dense[0].shape
    width = grad.shape[1]
    half = columns // 2
    step = 256
    per_side = half // step

    def place(i):
        side = i // per_side
        block = blocks[0] + side * (blocks[1] - blocks[0])
        part = parts[0] + side * (parts[1] - parts[0])
        return (block, 0, part * per_side + i % per_side)

    a_spec = pl.BlockSpec((1, rows, step), place)
    whole = pl.BlockSpec(memory_space=pltpu.VMEM)
    return pl.pallas_call(
        scatter_kernel,
        out_shape=(jax.ShapeDtypeStruct((half, width), F32),) * 2,
        grid=(2 * per_side,),
        in_specs=[whole, a_spec, a_spec] + [whole] * len(carried),
        out_specs=(whole, whole),
        compiler_params=params(MIB),
        cost_estimate=pl.CostEstimate(flops=flops, transcendentals=0, bytes_accessed=1),
        name="scatter_product",
    )(grad, dense[0], dense[1], *carried)


def per_device(features, weight, cotangent, tile_vals, col_tile, counts):
    size = lax.axis_size("row")
    hops = size // 2
    rep = lax.axis_index("rep")
    row = lax.axis_index("row")
    tiles_here = tile_vals.shape[0]
    width = features.shape[1] // 2
    half = features.shape[0] // 2
    ahead, back = ring_pairs(size)

    def forth(block):
        return lax.ppermute(block, "row", ahead)

    def rear(block):
        return lax.ppermute(block, "row", back)

    def swap(block):
        return lax.ppermute(block, "rep", [(0, 1), (1, 0)])

    def order(own, other, axis):
        low = jnp.where(rep == 0, own, other)
        high = jnp.where(rep == 0, other, own)
        return jnp.concatenate([low, high], axis)

    top = lax.dynamic_slice(features, (0, rep * width), (half, width))
    bottom = lax.dynamic_slice(features, (half, rep * width), (half, width))

    own_tiles = tile_vals[:, 0]
    other_tiles = swap(own_tiles)
    first_hop = (forth(top), rear(bottom))
    table = after(jnp.concatenate([col_tile[:, 0], counts], 1), *first_hop)
    tables = jnp.stack([table, swap(table)])
    columns = tables[:, :, :-1]
    block = jnp.mod(ring_place(columns // tiles_here, size) - ring_place(row, size), size)
    place = jnp.stack([block, columns % tiles_here], 1)
    count = tables[:, :, -1]

    w_own = jnp.where(rep == 0, weight[:width], weight[width:])
    w_other = jnp.where(rep == 0, weight[width:], weight[:width])
    w_rows = jnp.concatenate([w_own, w_other], 0)
    w_high = lax.reduce_precision(w_rows, 8, 7)
    w_hi, w_lo = w_high.astype(BF16), (w_rows - w_high).astype(BF16)

    dense, total = (), None
    cuts = [0, tiles_here * 3 // 8, tiles_here * 3 // 4, tiles_here]
    ready = []

    def next_piece():
        nonlocal dense
        done = next_piece.done
        if done < 3:
            dense = densify(
                dense, (own_tiles, other_tiles), place, count, size, cuts[done], cuts[done + 1]
            )
            next_piece.done += 1
            if next_piece.done < 3:
                return dense
        return multiply_ready()

    next_piece.done = 0

    def multiply_ready():
        nonlocal total
        if next_piece.done == 3 and ready:
            total = gather_product(dense[:2], ready.pop(0), total)
            return (total,)
        return ()

    ready.append([(0, top, bottom)])
    forward_top, forward_bottom, rear_top, rear_bottom = top, bottom, top, bottom
    covered = (w_hi, w_lo)
    for hop in range(1, hops + 1):
        if hop > 2:
            covered = next_piece()
        if hop > 1:
            forward_top, rear_bottom = (after(v, *covered) for v in (forward_top, rear_bottom))
            forward_top, rear_bottom = forth(forward_top), rear(rear_bottom)
        else:
            forward_top, rear_bottom = first_hop
        if hop < hops:
            if hop > 1:
                covered = next_piece()
                forward_bottom, rear_top = (after(v, *covered) for v in (forward_bottom, rear_top))
            forward_bottom = forth(forward_bottom)
            rear_top = rear(rear_top)
            ready.append(
                [(size - hop, forward_top, forward_bottom), (hop, rear_top, rear_bottom)]
            )
    while ready:
        multiply_ready()
    x_last = (forward_top, rear_bottom)
    other_total = swap(total)
    x_other = tuple(swap(v) for v in x_last)
    odd = jnp.mod(row, 2)
    output, pre_grad, weight_mine, weight_sent = layer(
        odd.reshape(1), dense[2:], x_last, x_other, total, other_total, cotangent, w_hi, w_lo
    )


    def exchange(block, distance):
        return lax.ppermute(block, "row", [(i, i ^ distance) for i in range(size)])

    weight_mine = weight_mine + exchange(weight_sent, 1)
    distance = 2
    while distance < size:
        weight_mine = weight_mine + exchange(weight_mine, distance)
        distance *= 2
    weight_theirs = exchange(weight_mine, 1)
    low = jnp.where(odd == 0, weight_mine, weight_theirs)
    high = jnp.where(odd == 0, weight_theirs, weight_mine)
    weight_half = jnp.concatenate([low, high], 0)
    grad, first_top, first_bottom = layer_grad(pre_grad, dense[2:], w_hi, w_lo)
    tops = (forth(first_top), rear(first_bottom))
    bottoms = ()
    for hop in range(hops - 1, 0, -1):
        blocks = (hop, size - hop)
        result = scatter_product(dense[:2], grad, blocks, (1, 0), bottoms)
        bottoms = (forth(result[0]), rear(result[1]))
        result = scatter_product(dense[:2], grad, blocks, (0, 1), tops)
        tops = (forth(result[0]), rear(result[1]))
    home_top, home_bottom = scatter_product(dense[:2], after(grad, *result), (0, 0), (0, 1))
    weight_grad = order(weight_half, swap(weight_half), 0)
    home_bottom = home_bottom + bottoms[0] + tops[1]
    home_top = home_top + bottoms[1] + tops[0]
    input_grad = jnp.concatenate(
        [order(home_top, swap(home_top), 1), order(home_bottom, swap(home_bottom), 1)], 0
    )
    return (output, input_grad, weight_grad)


def solution(mesh):
    return jax.shard_map(
        per_device,
        mesh=mesh,
        in_specs=(
            P(("groups", "row"), None),
            P(),
            P(("groups", "row"), None),
            P(("groups", "row"), "rep", None, None, None),
            P(("groups", "row"), "rep", None),
            P(("groups", "row"), "rep"),
        ),
        out_specs=(P(("groups", "row"), None), P(("groups", "row"), None), P("groups", None)),
        check_vma=False,
    )
```

```python
import functools

import jax
import jax.numpy as jnp
from jax import lax
from jax.experimental import pallas as pl
from jax.experimental.pallas import tpu as pltpu
from jax.sharding import PartitionSpec as P

BF16 = jnp.bfloat16
F32 = jnp.float32
MIB = 48
SP_FLOPS = [10_000_000_000, 1, 10_000_000_000, 1, 10_000_000_000, 1, 10_000_000_000]
LAYER_MIB = 40
SMALL = pl.CostEstimate(flops=10_000_000_000, transcendentals=0, bytes_accessed=8_000_000)


def ring_place(index, size):
    if size == 8:
        z, y = index // 2, index % 2
        return z + y * (size - 1 - 2 * z)
    return index


def ring_pairs(size):
    at = {ring_place(i, size): i for i in range(size)}
    ahead = [(at[p], at[(p + 1) % size]) for p in range(size)]
    back = [(b, a) for a, b in ahead]
    return ahead, back


def split_hi_lo(value):
    hi = value.astype(BF16)
    return hi, (value - hi.astype(F32)).astype(BF16)


def dot(a, b, dims=((1,), (0,))):
    return lax.dot_general(a, b, (dims, ((), ())), preferred_element_type=F32)


def params(mib):
    return pltpu.CompilerParams(vmem_limit_bytes=mib * 1024 * 1024)


def after(value, *others):
    return lax.optimization_barrier((value, *others))[0]


def densify_kernel(first, far, place_ref, count_ref, own_ref, other_ref, *refs):
    hi_ref, lo_ref, far_hi_ref, far_lo_ref = refs[-4:]
    row = first + pl.program_id(0)
    hi_ref[...] = jnp.zeros_like(hi_ref)
    lo_ref[...] = jnp.zeros_like(lo_ref)
    tile = own_ref.shape[-1]
    for replica, ref in enumerate((own_ref, other_ref)):

        def body(slot, carry, replica=replica, ref=ref):
            hi, lo = split_hi_lo(ref[0, slot])
            block = place_ref[replica, 0, row, slot]
            column = pl.multiple_of(place_ref[replica, 1, row, slot] * tile, tile)
            hi_ref[block, :, pl.ds(column, tile)] = hi
            lo_ref[block, :, pl.ds(column, tile)] = lo
            return carry

        lax.fori_loop(0, count_ref[replica, row], body, 0)
    far_hi_ref[...] = hi_ref[far]
    far_lo_ref[...] = lo_ref[far]


def densify(dense, tiles, place, count, size, first, last):
    own, other = tiles
    tiles_here, slots, tile, _ = own.shape
    rows = tiles_here * tile
    shape = jax.ShapeDtypeStruct((size, rows, rows), BF16)
    tile_spec = pl.BlockSpec((1, slots, tile, tile), lambda i, *_: (first + i, 0, 0, 0))
    out_spec = pl.BlockSpec((size, tile, rows), lambda i, *_: (0, first + i, 0))
    far_shape = jax.ShapeDtypeStruct((rows, rows), BF16)
    far_spec = pl.BlockSpec((tile, rows), lambda i, *_: (first + i, 0))
    return pl.pallas_call(
        functools.partial(densify_kernel, first, size // 2),
        out_shape=(shape, shape, far_shape, far_shape),
        grid_spec=pltpu.PrefetchScalarGridSpec(
            num_scalar_prefetch=2,
            grid=(last - first,),
            in_specs=[tile_spec, tile_spec] + [pl.BlockSpec(memory_space=pl.ANY)] * len(dense),
            out_specs=(out_spec, out_spec, far_spec, far_spec),
        ),
        input_output_aliases={4 + n: n for n in range(len(dense))},
        compiler_params=params(MIB),
        cost_estimate=pl.CostEstimate(
            flops=0,
            transcendentals=0,
            bytes_accessed=(last - first) * tile * (slots * tile * 8 + size * rows * 4),
        ),
        name="densify",
    )(place, count, own, other, *dense)


def gather_kernel(blocks, *refs):
    x_refs = refs[: 2 * blocks]
    a_refs = refs[2 * blocks : 4 * blocks]
    rest = refs[4 * blocks :]
    total_ref = rest[0] if len(rest) == 3 else None
    out_ref, x_split = rest[-2:]
    half, width = x_refs[0].shape

    @pl.when(pl.program_id(0) == 0)
    def _():
        for n in range(2 * blocks):
            hi, lo = split_hi_lo(x_refs[n][...])
            x_split[pl.ds(n * half, half), pl.ds(0, width)] = hi
            x_split[pl.ds(n * half, half), pl.ds(width, width)] = lo

    acc = None
    for n in range(blocks):
        span = pl.ds(n * 2 * half, 2 * half)
        both = dot(a_refs[2 * n][0], x_split[span, :])
        low = dot(a_refs[2 * n + 1][0], x_split[span, pl.ds(0, width)])
        part = both[:, :width] + both[:, width:] + low
        acc = part if acc is None else acc + part
    if total_ref is not None:
        acc = acc + total_ref[...]
    out_ref[...] = acc


def gather_product(dense, chunks, total):
    size, rows, columns = dense[0].shape
    half, width = chunks[0][1].shape
    blocks = len(chunks)
    step = rows // 2
    full = pl.BlockSpec((half, width), lambda i: (0, 0))
    in_specs = [full] * (2 * blocks)
    operands = [value for _, top, bottom in chunks for value in (top, bottom)]
    for block, _, _ in chunks:
        spec = pl.BlockSpec((1, step, columns), lambda i, block=block: (block, i, 0))
        in_specs += [spec, spec]
        operands += [dense[0], dense[1]]
    row_spec = pl.BlockSpec((step, width), lambda i: (i, 0))
    if total is not None:
        in_specs.append(row_spec)
        operands.append(total)
    return pl.pallas_call(
        functools.partial(gather_kernel, blocks),
        out_shape=jax.ShapeDtypeStruct((rows, width), F32),
        grid=(rows // step,),
        in_specs=in_specs,
        out_specs=row_spec,
        scratch_shapes=[pltpu.VMEM((blocks * 2 * half, 2 * width), BF16)],
        compiler_params=params(MIB),
        cost_estimate=pl.CostEstimate(
            flops=6 * blocks * rows * columns * width,
            transcendentals=0,
            bytes_accessed=blocks * (rows * columns * 4 + columns * width * 4) + rows * width * 8,
        ),
        name="gather_product",
    )(*operands)


def layer_kernel(*refs):
    odd_ref = refs[0]
    x_refs = refs[1:5]
    hi_ref, lo_ref, own_ref, other_ref, cot_ref, whi_ref, wlo_ref = refs[5:12]
    out_ref, pre_grad_ref, mine_ref, sent_ref, x_split, total_ref = refs[12:]
    half, width = x_refs[0].shape
    rows, columns = hi_ref.shape
    step = 512
    for n in range(4):
        hi, lo = split_hi_lo(x_refs[n][...])
        at, side = (n % 2) * half, pl.ds((n // 2) * width, width)
        x_split[pl.ds(at, half), side] = hi
        x_split[pl.ds(columns + at, half), side] = lo
        x_split[pl.ds(2 * columns + at, half), side] = hi
    for first in range(0, rows, step):
        here = pl.ds(first, step)
        hi, lo = hi_ref[here, :], lo_ref[here, :]
        total = dot(jnp.concatenate([hi, hi, lo], 1), x_split[...])
        total = total + jnp.concatenate([own_ref[here, :], other_ref[here, :]], 1)
        hi, lo = split_hi_lo(total)
        total_ref[here, :] = hi[:, :width]
        total_ref[pl.ds(rows + first, step), :] = lo[:, :width]
        w_hi, w_lo = whi_ref[...], wlo_ref[...]
        pre = dot(
            jnp.concatenate([hi, lo, hi], 1), jnp.concatenate([w_hi, w_hi, w_lo], 0)
        )
        sigma = jax.nn.sigmoid(pre)
        out_ref[here, :] = pre * sigma
        pre_grad = cot_ref[here, :] * (sigma * (1.0 + pre * (1.0 - sigma)))
        hi, lo = split_hi_lo(pre_grad)
        pre_grad_ref[here, :] = hi
        pre_grad_ref[pl.ds(rows + first, step), :] = lo
    value = turned_dot(total_ref[pl.ds(0, rows), :], total_ref[pl.ds(rows, rows), :], pre_grad_ref)
    top, bottom = value[: width // 2], value[width // 2 :]
    odd = odd_ref[0]
    mine_ref[...] = jnp.where(odd == 0, top, bottom)
    sent_ref[...] = jnp.where(odd == 0, bottom, top)


def layer_grad_kernel(*refs):
    pre_grad_ref, hi_ref, lo_ref, whi_ref, wlo_ref, grad_ref, top_ref, bottom_ref = refs
    rows = hi_ref.shape[0]
    half, width = top_ref.shape
    step = 512
    mine = pl.ds(0, width)
    for first in range(0, rows, step):
        hi, lo = pre_grad_ref[pl.ds(first, step), :], pre_grad_ref[pl.ds(rows + first, step), :]
        w_hi, w_lo = whi_ref[mine, :], wlo_ref[mine, :]
        grad = dot(
            jnp.concatenate([hi, lo, hi], 1),
            jnp.concatenate([w_hi, w_hi, w_lo], 1),
            ((1,), (1,)),
        )
        hi, lo = split_hi_lo(grad)
        grad_ref[pl.ds(first, step), :] = hi
        grad_ref[pl.ds(rows + first, step), :] = lo
    for first in range(0, 2 * half, 256):
        part = turned_dot(hi_ref[:, pl.ds(first, 256)], lo_ref[:, pl.ds(first, 256)], grad_ref)
        if first < half:
            top_ref[pl.ds(first, 256), :] = part
        else:
            bottom_ref[pl.ds(first - half, 256), :] = part


def turned_dot(hi, lo, right_ref):
    rows = hi.shape[0]
    right_hi, right_lo = right_ref[pl.ds(0, rows), :], right_ref[pl.ds(rows, rows), :]
    left = jnp.concatenate([hi, hi, lo], 0)
    return dot(left, jnp.concatenate([right_hi, right_lo, right_hi], 0), ((0,), (0,)))


def layer(odd, far, x_own, x_other, own, other, cotangent, w_hi, w_lo):
    rows, columns = far[0].shape
    width = own.shape[1]
    features = cotangent.shape[1]
    whole = pl.BlockSpec(memory_space=pltpu.VMEM)
    return pl.pallas_call(
        layer_kernel,
        out_shape=(
            jax.ShapeDtypeStruct((rows, features), F32),
            jax.ShapeDtypeStruct((2 * rows, features), BF16),
            jax.ShapeDtypeStruct((width // 2, features), F32),
            jax.ShapeDtypeStruct((width // 2, features), F32),
        ),
        in_specs=[pl.BlockSpec(memory_space=pltpu.SMEM)] + [whole] * 11,
        out_specs=(whole,) * 4,
        scratch_shapes=[
            pltpu.VMEM((3 * columns, features), BF16),
            pltpu.VMEM((2 * rows, width), BF16),
        ],
        compiler_params=params(LAYER_MIB),
        cost_estimate=pl.CostEstimate(flops=1, transcendentals=0, bytes_accessed=1),
        name="layer",
    )(odd, *x_own, *x_other, *far, own, other, cotangent, w_hi, w_lo)


def layer_grad(pre_grad, far, w_hi, w_lo):
    rows, columns = far[0].shape
    width = w_hi.shape[0] // 2
    whole = pl.BlockSpec(memory_space=pltpu.VMEM)
    return pl.pallas_call(
        layer_grad_kernel,
        out_shape=(
            jax.ShapeDtypeStruct((2 * rows, width), BF16),
            jax.ShapeDtypeStruct((columns // 2, width), F32),
            jax.ShapeDtypeStruct((columns // 2, width), F32),
        ),
        in_specs=[whole] * 5,
        out_specs=(whole,) * 3,
        compiler_params=params(LAYER_MIB),
        cost_estimate=pl.CostEstimate(flops=10000000000, transcendentals=0, bytes_accessed=1),
        name="layer_grad",
    )(pre_grad, *far, w_hi, w_lo)


def scatter_kernel(*refs):
    grad_ref, hi_ref, lo_ref = refs[:3]
    came, outs = refs[3:-2], refs[-2:]
    part = turned_dot(hi_ref[0], lo_ref[0], grad_ref)
    step = part.shape[0]
    per_side = outs[0].shape[0] // step
    at = pl.program_id(0)
    for side in range(2):

        @pl.when(at // per_side == side)
        def _(side=side):
            here = pl.ds((at % per_side) * step, step)
            outs[side][here, :] = part + came[side][here, :] if came else part


def scatter_product(dense, grad, blocks, parts, carried=()):
    flops = SP_FLOPS[(0 if blocks[0] == 0 else (6 - 2 * blocks[0]) + (2 if parts[0] == 0 else 1)) if dense[0].shape[0] == 8 else 0]
    size, rows, columns = dense[0].shape
    width = grad.shape[1]
    half = columns // 2
    step = 256
    per_side = half // step

    def place(i):
        side = i // per_side
        block = blocks[0] + side * (blocks[1] - blocks[0])
        part = parts[0] + side * (parts[1] - parts[0])
        return (block, 0, part * per_side + i % per_side)

    a_spec = pl.BlockSpec((1, rows, step), place)
    whole = pl.BlockSpec(memory_space=pltpu.VMEM)
    return pl.pallas_call(
        scatter_kernel,
        out_shape=(jax.ShapeDtypeStruct((half, width), F32),) * 2,
        grid=(2 * per_side,),
        in_specs=[whole, a_spec, a_spec] + [whole] * len(carried),
        out_specs=(whole, whole),
        compiler_params=params(MIB),
        cost_estimate=pl.CostEstimate(flops=flops, transcendentals=0, bytes_accessed=1),
        name="scatter_product",
    )(grad, dense[0], dense[1], *carried)


def per_device(features, weight, cotangent, tile_vals, col_tile, counts):
    size = lax.axis_size("row")
    hops = size // 2
    rep = lax.axis_index("rep")
    row = lax.axis_index("row")
    tiles_here = tile_vals.shape[0]
    width = features.shape[1] // 2
    half = features.shape[0] // 2
    ahead, back = ring_pairs(size)

    def forth(block):
        return lax.ppermute(block, "row", ahead)

    def rear(block):
        return lax.ppermute(block, "row", back)

    def swap(block):
        return lax.ppermute(block, "rep", [(0, 1), (1, 0)])

    def order(own, other, axis):
        low = jnp.where(rep == 0, own, other)
        high = jnp.where(rep == 0, other, own)
        return jnp.concatenate([low, high], axis)

    top = lax.dynamic_slice(features, (0, rep * width), (half, width))
    bottom = lax.dynamic_slice(features, (half, rep * width), (half, width))

    own_tiles = tile_vals[:, 0]
    other_tiles = swap(own_tiles)
    first_hop = (forth(top), rear(bottom))
    table = after(jnp.concatenate([col_tile[:, 0], counts], 1), *first_hop)
    tables = jnp.stack([table, swap(table)])
    columns = tables[:, :, :-1]
    block = jnp.mod(ring_place(columns // tiles_here, size) - ring_place(row, size), size)
    place = jnp.stack([block, columns % tiles_here], 1)
    count = tables[:, :, -1]

    w_own = jnp.where(rep == 0, weight[:width], weight[width:])
    w_other = jnp.where(rep == 0, weight[width:], weight[:width])
    w_rows = jnp.concatenate([w_own, w_other], 0)
    w_high = lax.reduce_precision(w_rows, 8, 7)
    w_hi, w_lo = w_high.astype(BF16), (w_rows - w_high).astype(BF16)

    dense, total = (), None
    cuts = [0, tiles_here * 3 // 8, tiles_here * 3 // 4, tiles_here]
    ready = []

    def next_piece():
        nonlocal dense
        done = next_piece.done
        if done < 3:
            dense = densify(
                dense, (own_tiles, other_tiles), place, count, size, cuts[done], cuts[done + 1]
            )
            next_piece.done += 1
            if next_piece.done < 3:
                return dense
        return multiply_ready()

    next_piece.done = 0

    def multiply_ready():
        nonlocal total
        if next_piece.done == 3 and ready:
            total = gather_product(dense[:2], ready.pop(0), total)
            return (total,)
        return ()

    ready.append([(0, top, bottom)])
    forward_top, forward_bottom, rear_top, rear_bottom = top, bottom, top, bottom
    covered = (w_hi, w_lo)
    for hop in range(1, hops + 1):
        if hop > 2:
            covered = next_piece()
        if hop > 1:
            forward_top, rear_bottom = (after(v, *covered) for v in (forward_top, rear_bottom))
            forward_top, rear_bottom = forth(forward_top), rear(rear_bottom)
        else:
            forward_top, rear_bottom = first_hop
        if hop < hops:
            if hop > 1:
                covered = next_piece()
                forward_bottom, rear_top = (after(v, *covered) for v in (forward_bottom, rear_top))
            forward_bottom = forth(forward_bottom)
            rear_top = rear(rear_top)
            ready.append(
                [(size - hop, forward_top, forward_bottom), (hop, rear_top, rear_bottom)]
            )
    while ready:
        multiply_ready()
    x_last = (forward_top, rear_bottom)
    other_total = swap(total)
    x_other = tuple(swap(v) for v in x_last)
    odd = jnp.mod(row, 2)
    output, pre_grad, weight_mine, weight_sent = layer(
        odd.reshape(1), dense[2:], x_last, x_other, total, other_total, cotangent, w_hi, w_lo
    )


    def exchange(block, distance):
        return lax.ppermute(block, "row", [(i, i ^ distance) for i in range(size)])

    weight_mine = weight_mine + exchange(weight_sent, 1)
    near_odd = jnp.mod(row // 2, 2)
    quarter = weight_mine.shape[0] // 2
    weight_sent = lax.dynamic_slice_in_dim(weight_mine, (1 - near_odd) * quarter, quarter, 0)
    weight_part = lax.dynamic_slice_in_dim(weight_mine, near_odd * quarter, quarter, 0)
    weight_part = weight_part + exchange(weight_sent, 2)
    distance = 4
    while distance < size:
        weight_part = weight_part + exchange(weight_part, distance)
        distance *= 2
    weight_rest = exchange(weight_part, 2)
    low = jnp.where(near_odd == 0, weight_part, weight_rest)
    high = jnp.where(near_odd == 0, weight_rest, weight_part)
    weight_mine = jnp.concatenate([low, high], 0)
    weight_theirs = exchange(weight_mine, 1)
    low = jnp.where(odd == 0, weight_mine, weight_theirs)
    high = jnp.where(odd == 0, weight_theirs, weight_mine)
    weight_half = jnp.concatenate([low, high], 0)
    grad, first_top, first_bottom = layer_grad(pre_grad, dense[2:], w_hi, w_lo)
    tops = (forth(first_top), rear(first_bottom))
    bottoms = ()
    for hop in range(hops - 1, 0, -1):
        blocks = (hop, size - hop)
        result = scatter_product(dense[:2], grad, blocks, (1, 0), bottoms)
        bottoms = (forth(result[0]), rear(result[1]))
        result = scatter_product(dense[:2], grad, blocks, (0, 1), tops)
        tops = (forth(result[0]), rear(result[1]))
    home_top, home_bottom = scatter_product(dense[:2], after(grad, *result), (0, 0), (0, 1))
    weight_grad = order(weight_half, swap(weight_half), 0)
    home_bottom = home_bottom + bottoms[0] + tops[1]
    home_top = home_top + bottoms[1] + tops[0]
    input_grad = jnp.concatenate(
        [order(home_top, swap(home_top), 1), order(home_bottom, swap(home_bottom), 1)], 0
    )
    return (output, input_grad, weight_grad)


def solution(mesh):
    return jax.shard_map(
        per_device,
        mesh=mesh,
        in_specs=(
            P(("groups", "row"), None),
            P(),
            P(("groups", "row"), None),
            P(("groups", "row"), "rep", None, None, None),
            P(("groups", "row"), "rep", None),
            P(("groups", "row"), "rep"),
        ),
        out_specs=(P(("groups", "row"), None), P(("groups", "row"), None), P("groups", None)),
        check_vma=False,
    )
```

```python
import functools

import jax
import jax.numpy as jnp
from jax import lax
from jax.experimental import pallas as pl
from jax.experimental.pallas import tpu as pltpu
from jax.sharding import PartitionSpec as P

BF16 = jnp.bfloat16
F32 = jnp.float32
MIB = 48
SP_FLOPS = [10_000_000_000, 1, 10_000_000_000, 1, 10_000_000_000, 1, 10_000_000_000]
LAYER_MIB = 40
SMALL = pl.CostEstimate(flops=10_000_000_000, transcendentals=0, bytes_accessed=8_000_000)


def ring_place(index, size):
    if size == 8:
        z, y = index // 2, index % 2
        return z + y * (size - 1 - 2 * z)
    return index


def ring_pairs(size):
    at = {ring_place(i, size): i for i in range(size)}
    ahead = [(at[p], at[(p + 1) % size]) for p in range(size)]
    back = [(b, a) for a, b in ahead]
    return ahead, back


def split_hi_lo(value):
    hi = value.astype(BF16)
    return hi, (value - hi.astype(F32)).astype(BF16)


def dot(a, b, dims=((1,), (0,))):
    return lax.dot_general(a, b, (dims, ((), ())), preferred_element_type=F32)


def params(mib):
    return pltpu.CompilerParams(vmem_limit_bytes=mib * 1024 * 1024)


def after(value, *others):
    return lax.optimization_barrier((value, *others))[0]


def densify_kernel(first, far, place_ref, count_ref, own_ref, other_ref, *refs):
    hi_ref, lo_ref, far_hi_ref, far_lo_ref = refs[-4:]
    row = first + pl.program_id(0)
    hi_ref[...] = jnp.zeros_like(hi_ref)
    lo_ref[...] = jnp.zeros_like(lo_ref)
    tile = own_ref.shape[-1]
    for replica, ref in enumerate((own_ref, other_ref)):

        def body(slot, carry, replica=replica, ref=ref):
            hi, lo = split_hi_lo(ref[0, slot])
            block = place_ref[replica, 0, row, slot]
            column = pl.multiple_of(place_ref[replica, 1, row, slot] * tile, tile)
            hi_ref[block, :, pl.ds(column, tile)] = hi
            lo_ref[block, :, pl.ds(column, tile)] = lo
            return carry

        lax.fori_loop(0, count_ref[replica, row], body, 0)
    far_hi_ref[...] = hi_ref[far]
    far_lo_ref[...] = lo_ref[far]


def densify(dense, tiles, place, count, size, first, last):
    own, other = tiles
    tiles_here, slots, tile, _ = own.shape
    rows = tiles_here * tile
    shape = jax.ShapeDtypeStruct((size, rows, rows), BF16)
    tile_spec = pl.BlockSpec((1, slots, tile, tile), lambda i, *_: (first + i, 0, 0, 0))
    out_spec = pl.BlockSpec((size, tile, rows), lambda i, *_: (0, first + i, 0))
    far_shape = jax.ShapeDtypeStruct((rows, rows), BF16)
    far_spec = pl.BlockSpec((tile, rows), lambda i, *_: (first + i, 0))
    return pl.pallas_call(
        functools.partial(densify_kernel, first, size // 2),
        out_shape=(shape, shape, far_shape, far_shape),
        grid_spec=pltpu.PrefetchScalarGridSpec(
            num_scalar_prefetch=2,
            grid=(last - first,),
            in_specs=[tile_spec, tile_spec] + [pl.BlockSpec(memory_space=pl.ANY)] * len(dense),
            out_specs=(out_spec, out_spec, far_spec, far_spec),
        ),
        input_output_aliases={4 + n: n for n in range(len(dense))},
        compiler_params=params(MIB),
        cost_estimate=pl.CostEstimate(
            flops=0,
            transcendentals=0,
            bytes_accessed=(last - first) * tile * (slots * tile * 8 + size * rows * 4),
        ),
        name="densify",
    )(place, count, own, other, *dense)


def gather_kernel(blocks, *refs):
    x_refs = refs[: 2 * blocks]
    a_refs = refs[2 * blocks : 4 * blocks]
    rest = refs[4 * blocks :]
    total_ref = rest[0] if len(rest) == 3 else None
    out_ref, x_split = rest[-2:]
    half, width = x_refs[0].shape

    @pl.when(pl.program_id(0) == 0)
    def _():
        for n in range(2 * blocks):
            hi, lo = split_hi_lo(x_refs[n][...])
            x_split[pl.ds(n * half, half), pl.ds(0, width)] = hi
            x_split[pl.ds(n * half, half), pl.ds(width, width)] = lo

    acc = None
    for n in range(blocks):
        span = pl.ds(n * 2 * half, 2 * half)
        both = dot(a_refs[2 * n][0], x_split[span, :])
        low = dot(a_refs[2 * n + 1][0], x_split[span, pl.ds(0, width)])
        part = both[:, :width] + both[:, width:] + low
        acc = part if acc is None else acc + part
    if total_ref is not None:
        acc = acc + total_ref[...]
    out_ref[...] = acc


def gather_product(dense, chunks, total):
    size, rows, columns = dense[0].shape
    half, width = chunks[0][1].shape
    blocks = len(chunks)
    step = rows // 2
    full = pl.BlockSpec((half, width), lambda i: (0, 0))
    in_specs = [full] * (2 * blocks)
    operands = [value for _, top, bottom in chunks for value in (top, bottom)]
    for block, _, _ in chunks:
        spec = pl.BlockSpec((1, step, columns), lambda i, block=block: (block, i, 0))
        in_specs += [spec, spec]
        operands += [dense[0], dense[1]]
    row_spec = pl.BlockSpec((step, width), lambda i: (i, 0))
    if total is not None:
        in_specs.append(row_spec)
        operands.append(total)
    return pl.pallas_call(
        functools.partial(gather_kernel, blocks),
        out_shape=jax.ShapeDtypeStruct((rows, width), F32),
        grid=(rows // step,),
        in_specs=in_specs,
        out_specs=row_spec,
        scratch_shapes=[pltpu.VMEM((blocks * 2 * half, 2 * width), BF16)],
        compiler_params=params(MIB),
        cost_estimate=pl.CostEstimate(
            flops=6 * blocks * rows * columns * width,
            transcendentals=0,
            bytes_accessed=blocks * (rows * columns * 4 + columns * width * 4) + rows * width * 8,
        ),
        name="gather_product",
    )(*operands)


def layer_kernel(*refs):
    odd_ref = refs[0]
    x_refs = refs[1:5]
    hi_ref, lo_ref, own_ref, other_ref, cot_ref, whi_ref, wlo_ref = refs[5:12]
    out_ref, pre_grad_ref, mine_ref, sent_ref, x_split, total_ref = refs[12:]
    half, width = x_refs[0].shape
    rows, columns = hi_ref.shape
    step = 512
    for n in range(4):
        hi, lo = split_hi_lo(x_refs[n][...])
        at, side = (n % 2) * half, pl.ds((n // 2) * width, width)
        x_split[pl.ds(at, half), side] = hi
        x_split[pl.ds(columns + at, half), side] = lo
        x_split[pl.ds(2 * columns + at, half), side] = hi
    for first in range(0, rows, step):
        here = pl.ds(first, step)
        hi, lo = hi_ref[here, :], lo_ref[here, :]
        total = dot(jnp.concatenate([hi, hi, lo], 1), x_split[...])
        total = total + jnp.concatenate([own_ref[here, :], other_ref[here, :]], 1)
        hi, lo = split_hi_lo(total)
        total_ref[here, :] = hi[:, :width]
        total_ref[pl.ds(rows + first, step), :] = lo[:, :width]
        w_hi, w_lo = whi_ref[...], wlo_ref[...]
        pre = dot(
            jnp.concatenate([hi, lo, hi], 1), jnp.concatenate([w_hi, w_hi, w_lo], 0)
        )
        sigma = jax.nn.sigmoid(pre)
        out_ref[here, :] = pre * sigma
        pre_grad = cot_ref[here, :] * (sigma * (1.0 + pre * (1.0 - sigma)))
        hi, lo = split_hi_lo(pre_grad)
        pre_grad_ref[here, :] = hi
        pre_grad_ref[pl.ds(rows + first, step), :] = lo
    value = turned_dot(total_ref[pl.ds(0, rows), :], total_ref[pl.ds(rows, rows), :], pre_grad_ref)
    top, bottom = value[: width // 2], value[width // 2 :]
    odd = odd_ref[0]
    mine_ref[...] = jnp.where(odd == 0, top, bottom)
    sent_ref[...] = jnp.where(odd == 0, bottom, top)


def layer_grad_kernel(*refs):
    pre_grad_ref, hi_ref, lo_ref, whi_ref, wlo_ref, grad_ref, top_ref, bottom_ref = refs
    rows = hi_ref.shape[0]
    half, width = top_ref.shape
    step = 512
    mine = pl.ds(0, width)
    for first in range(0, rows, step):
        hi, lo = pre_grad_ref[pl.ds(first, step), :], pre_grad_ref[pl.ds(rows + first, step), :]
        w_hi, w_lo = whi_ref[mine, :], wlo_ref[mine, :]
        grad = dot(
            jnp.concatenate([hi, lo, hi], 1),
            jnp.concatenate([w_hi, w_hi, w_lo], 1),
            ((1,), (1,)),
        )
        hi, lo = split_hi_lo(grad)
        grad_ref[pl.ds(first, step), :] = hi
        grad_ref[pl.ds(rows + first, step), :] = lo
    for first in range(0, 2 * half, 256):
        part = turned_dot(hi_ref[:, pl.ds(first, 256)], lo_ref[:, pl.ds(first, 256)], grad_ref)
        if first < half:
            top_ref[pl.ds(first, 256), :] = part
        else:
            bottom_ref[pl.ds(first - half, 256), :] = part


def turned_dot(hi, lo, right_ref):
    rows = hi.shape[0]
    right_hi, right_lo = right_ref[pl.ds(0, rows), :], right_ref[pl.ds(rows, rows), :]
    left = jnp.concatenate([hi, hi, lo], 0)
    return dot(left, jnp.concatenate([right_hi, right_lo, right_hi], 0), ((0,), (0,)))


def layer(odd, far, x_own, x_other, own, other, cotangent, w_hi, w_lo):
    rows, columns = far[0].shape
    width = own.shape[1]
    features = cotangent.shape[1]
    whole = pl.BlockSpec(memory_space=pltpu.VMEM)
    return pl.pallas_call(
        layer_kernel,
        out_shape=(
            jax.ShapeDtypeStruct((rows, features), F32),
            jax.ShapeDtypeStruct((2 * rows, features), BF16),
            jax.ShapeDtypeStruct((width // 2, features), F32),
            jax.ShapeDtypeStruct((width // 2, features), F32),
        ),
        in_specs=[pl.BlockSpec(memory_space=pltpu.SMEM)] + [whole] * 11,
        out_specs=(whole,) * 4,
        scratch_shapes=[
            pltpu.VMEM((3 * columns, features), BF16),
            pltpu.VMEM((2 * rows, width), BF16),
        ],
        compiler_params=params(LAYER_MIB),
        cost_estimate=pl.CostEstimate(flops=1, transcendentals=0, bytes_accessed=1),
        name="layer",
    )(odd, *x_own, *x_other, *far, own, other, cotangent, w_hi, w_lo)


def layer_grad(pre_grad, far, w_hi, w_lo):
    rows, columns = far[0].shape
    width = w_hi.shape[0] // 2
    whole = pl.BlockSpec(memory_space=pltpu.VMEM)
    return pl.pallas_call(
        layer_grad_kernel,
        out_shape=(
            jax.ShapeDtypeStruct((2 * rows, width), BF16),
            jax.ShapeDtypeStruct((columns // 2, width), F32),
            jax.ShapeDtypeStruct((columns // 2, width), F32),
        ),
        in_specs=[whole] * 5,
        out_specs=(whole,) * 3,
        compiler_params=params(LAYER_MIB),
        cost_estimate=pl.CostEstimate(flops=10000000000, transcendentals=0, bytes_accessed=1),
        name="layer_grad",
    )(pre_grad, *far, w_hi, w_lo)


def scatter_kernel(*refs):
    grad_ref, hi_ref, lo_ref = refs[:3]
    came, outs = refs[3:-2], refs[-2:]
    part = turned_dot(hi_ref[0], lo_ref[0], grad_ref)
    step = part.shape[0]
    per_side = outs[0].shape[0] // step
    at = pl.program_id(0)
    for side in range(2):

        @pl.when(at // per_side == side)
        def _(side=side):
            here = pl.ds((at % per_side) * step, step)
            outs[side][here, :] = part + came[side][here, :] if came else part


def scatter_product(dense, grad, blocks, parts, carried=()):
    flops = SP_FLOPS[(0 if blocks[0] == 0 else (6 - 2 * blocks[0]) + (2 if parts[0] == 0 else 1)) if dense[0].shape[0] == 8 else 0]
    size, rows, columns = dense[0].shape
    width = grad.shape[1]
    half = columns // 2
    step = 256
    per_side = half // step

    def place(i):
        side = i // per_side
        block = blocks[0] + side * (blocks[1] - blocks[0])
        part = parts[0] + side * (parts[1] - parts[0])
        return (block, 0, part * per_side + i % per_side)

    a_spec = pl.BlockSpec((1, rows, step), place)
    whole = pl.BlockSpec(memory_space=pltpu.VMEM)
    return pl.pallas_call(
        scatter_kernel,
        out_shape=(jax.ShapeDtypeStruct((half, width), F32),) * 2,
        grid=(2 * per_side,),
        in_specs=[whole, a_spec, a_spec] + [whole] * len(carried),
        out_specs=(whole, whole),
        compiler_params=params(MIB),
        cost_estimate=pl.CostEstimate(flops=flops, transcendentals=0, bytes_accessed=1),
        name="scatter_product",
    )(grad, dense[0], dense[1], *carried)


def per_device(features, weight, cotangent, tile_vals, col_tile, counts):
    size = lax.axis_size("row")
    hops = size // 2
    rep = lax.axis_index("rep")
    row = lax.axis_index("row")
    tiles_here = tile_vals.shape[0]
    width = features.shape[1] // 2
    half = features.shape[0] // 2
    ahead, back = ring_pairs(size)

    def forth(block):
        return lax.ppermute(block, "row", ahead)

    def rear(block):
        return lax.ppermute(block, "row", back)

    def swap(block):
        return lax.ppermute(block, "rep", [(0, 1), (1, 0)])

    def order(own, other, axis):
        low = jnp.where(rep == 0, own, other)
        high = jnp.where(rep == 0, other, own)
        return jnp.concatenate([low, high], axis)

    top = lax.dynamic_slice(features, (0, rep * width), (half, width))
    bottom = lax.dynamic_slice(features, (half, rep * width), (half, width))

    own_tiles = tile_vals[:, 0]
    other_tiles = swap(own_tiles)
    first_hop = (forth(top), rear(bottom))
    table = after(jnp.concatenate([col_tile[:, 0], counts], 1), *first_hop)
    tables = jnp.stack([table, swap(table)])
    columns = tables[:, :, :-1]
    block = jnp.mod(ring_place(columns // tiles_here, size) - ring_place(row, size), size)
    place = jnp.stack([block, columns % tiles_here], 1)
    count = tables[:, :, -1]

    w_own = jnp.where(rep == 0, weight[:width], weight[width:])
    w_other = jnp.where(rep == 0, weight[width:], weight[:width])
    w_rows = jnp.concatenate([w_own, w_other], 0)
    w_high = lax.reduce_precision(w_rows, 8, 7)
    w_hi, w_lo = w_high.astype(BF16), (w_rows - w_high).astype(BF16)

    dense, total = (), None
    cuts = [0, tiles_here * 3 // 8, tiles_here * 3 // 4, tiles_here]
    ready = []

    def next_piece():
        nonlocal dense
        done = next_piece.done
        if done < 3:
            dense = densify(
                dense, (own_tiles, other_tiles), place, count, size, cuts[done], cuts[done + 1]
            )
            next_piece.done += 1
            if next_piece.done < 3:
                return dense
        return multiply_ready()

    next_piece.done = 0

    def multiply_ready():
        nonlocal total
        if next_piece.done == 3 and ready:
            total = gather_product(dense[:2], ready.pop(0), total)
            return (total,)
        return ()

    ready.append([(0, top, bottom)])
    forward_top, forward_bottom, rear_top, rear_bottom = top, bottom, top, bottom
    covered = (w_hi, w_lo)
    for hop in range(1, hops + 1):
        if hop > 2:
            covered = next_piece()
        if hop > 1:
            forward_top, rear_bottom = (after(v, *covered) for v in (forward_top, rear_bottom))
            forward_top, rear_bottom = forth(forward_top), rear(rear_bottom)
        else:
            forward_top, rear_bottom = first_hop
        if hop < hops:
            if hop > 1:
                covered = next_piece()
                forward_bottom, rear_top = (after(v, *covered) for v in (forward_bottom, rear_top))
            forward_bottom = forth(forward_bottom)
            rear_top = rear(rear_top)
            ready.append(
                [(size - hop, forward_top, forward_bottom), (hop, rear_top, rear_bottom)]
            )
    while ready:
        multiply_ready()
    x_last = (forward_top, rear_bottom)
    other_total = swap(total)
    x_other = tuple(swap(v) for v in x_last)
    odd = jnp.mod(row, 2)
    output, pre_grad, weight_mine, weight_sent = layer(
        odd.reshape(1), dense[2:], x_last, x_other, total, other_total, cotangent, w_hi, w_lo
    )


    def exchange(block, distance):
        return lax.ppermute(block, "row", [(i, i ^ distance) for i in range(size)])

    weight_mine = weight_mine + exchange(weight_sent, 1)
    near_odd = jnp.mod(row // 2, 2)
    quarter = weight_mine.shape[0] // 2
    weight_sent = lax.dynamic_slice_in_dim(weight_mine, (1 - near_odd) * quarter, quarter, 0)
    weight_part = lax.dynamic_slice_in_dim(weight_mine, near_odd * quarter, quarter, 0)
    weight_part = weight_part + exchange(weight_sent, 2)
    distance = 4
    while distance < size:
        weight_part = weight_part + exchange(weight_part, distance)
        distance *= 2
    weight_rest = exchange(weight_part, 2)
    low = jnp.where(near_odd == 0, weight_part, weight_rest)
    high = jnp.where(near_odd == 0, weight_rest, weight_part)
    weight_mine = jnp.concatenate([low, high], 0)
    weight_theirs = exchange(weight_mine, 1)
    low = jnp.where(odd == 0, weight_mine, weight_theirs)
    high = jnp.where(odd == 0, weight_theirs, weight_mine)
    weight_half = jnp.concatenate([low, high], 0)
    grad, first_top, first_bottom = layer_grad(pre_grad, dense[2:], w_hi, w_lo)
    tops = (forth(first_top), rear(first_bottom))
    bottoms = ()
    for hop in range(hops - 1, 0, -1):
        blocks = (hop, size - hop)
        result = scatter_product(dense[:2], grad, blocks, (1, 0), bottoms)
        bottoms = (forth(result[0]), rear(result[1]))
        result = scatter_product(dense[:2], grad, blocks, (0, 1), tops)
        tops = (forth(result[0]), rear(result[1]))
    home_top, home_bottom = scatter_product(dense[:2], after(grad, *result), (0, 0), (0, 1))
    weight_grad = order(weight_half, swap(weight_half), 0)
    early = (home_top + bottoms[1], home_bottom + bottoms[0])
    other_early = tuple(swap(v) for v in early)
    other_tops = tuple(swap(v) for v in tops)
    input_grad = jnp.concatenate(
        [
            order(early[n] + tops[n], other_early[n] + other_tops[n], 1)
            for n in range(2)
        ],
        0,
    )
    return (output, input_grad, weight_grad)


def solution(mesh):
    return jax.shard_map(
        per_device,
        mesh=mesh,
        in_specs=(
            P(("groups", "row"), None),
            P(),
            P(("groups", "row"), None),
            P(("groups", "row"), "rep", None, None, None),
            P(("groups", "row"), "rep", None),
            P(("groups", "row"), "rep"),
        ),
        out_specs=(P(("groups", "row"), None), P(("groups", "row"), None), P("groups", None)),
        check_vma=False,
    )
```
